128 devices in a mesh: pop: 8 (over x, core), unit: 16 (over z, y).
Axes of the slice: x: 4, y: 4, z: 4, core: 2. Of those that a mesh axis runs over, the one named last changes fastest.
Arguments:
- states: bfloat16 [4, 4096, 1024], P(None, 'unit', 'pop'), may hold values from -6 to 6
- gate_inputs: bfloat16 [4, 3, 4096, 1024], P(None, None, 'unit', 'pop'), may hold values from -6 to 6
- actions: bfloat16 [4, 128, 1024], P(None, None, 'pop'), may hold values from -0.8984375 to 0.8984375
- final_grad: bfloat16 [4096, 1024], P('unit', 'pop'), may hold values from -6 to 6
- recur_weight: bfloat16 [4096, 3, 4096], P(None, None, 'unit'), may hold values from -0.09375 to 0.09375
- act_weight: bfloat16 [128, 3, 4096], P(None, None, 'unit'), may hold values from -0.5 to 0.5
- opp_first: bfloat16 [32, 4096, 4096], P('pop', None, 'unit'), may hold values from -0.09375 to 0.09375
- opp_second: bfloat16 [32, 128, 4096], P('pop'), may hold values from -0.09375 to 0.09375
- opponent: int32 [1024, 1], P('pop'), may hold values from 0 to 31; in each aligned block of 128 rows (0 to 127, 128 to 255, ...) at most 12 rows name the same one
Outputs:
- start_grad: bfloat16 [4096, 1024], P('unit', 'pop')
- act_weight_grad: float32 [128, 3, 4096], P(None, None, 'unit')
The draws below stay inside these ranges and needn't reach their ends.
Inputs may be any that keep to these rules, and one draw needn't show every extreme that they name: In each aligned block of 128 rows (the rows of one index of pop) no opponent is named by more than 12 rows, a bound that some block reaches.
All inputs are finite; a program needn't handle non-finite values.
Results may differ from the reference program's by a relative error of at most 0.02.
Values may be sent and summed in bfloat16 or wider, within the bound.
A program may use at most 128 MiB of HBM per device.

```python
import math
import jax
import jax.numpy as jnp
import numpy as np
from jax import lax

H = 4096
HID = 4096
A = 128
MEMBERS = 32
STEPS = 4
R_DEV = 128
CAP = 12
ROWS = 1024
N_POP = 8
N_UNIT = 16


def shard_levels(own_key, shape, split, least, top_value):
    def one(dim, blocks):
        draws = jax.random.uniform(jax.random.fold_in(jax.random.fold_in(own_key, 6), dim), (blocks,), jnp.float32, least / len(split), top_value / len(split))
        return jnp.repeat(jnp.exp(draws), shape[dim] // blocks).reshape((-1,) + (1,) * (len(shape) - dim - 1))

    factor_of = one(*split[0])
    for cut in split[1:]:
        factor_of = factor_of * one(*cut)
    return factor_of


def assign_block(stream_key, own, number, rows, amount, top, bound, lean):
    order = jax.random.permutation(stream_key, amount)
    heavy_load, usual = portions_of(amount, rows * top, bound, lean, True), portions_of(amount, rows * top, bound, lean, False)
    places = jnp.arange(amount)

    def named(tallies, turn):
        used = int((tallies > 0).sum())
        fixed = max(1, used // 4)
        passed = fixed + (places - fixed + turn * (used - fixed)) % max(1, amount - fixed)
        return jnp.zeros((amount,), jnp.int32).at[order[jnp.where(places < fixed, places, passed)]].set(jnp.asarray(tallies, jnp.int32))

    tallies = jnp.where(number % 4 == 0, named(heavy_load, number // 4), named(usual, number - number // 4 - 1))
    mixed = jax.random.permutation(jax.random.fold_in(own, 3), amount)
    giver, receiver = mixed[0:amount // 2 * 2:2], mixed[1:amount // 2 * 2:2]
    room = jnp.minimum(tallies[giver] - 1, bound - tallies[receiver]) // 2
    room = jnp.where((giver == order[0]) | (receiver == order[0]) | (tallies[receiver] == 0), 0, jnp.maximum(room, 0))
    passed = jax.random.randint(jax.random.fold_in(own, 4), (amount // 2,), 0, 1 << 20) % (room + 1)
    tallies = tallies.at[giver].add(-passed).at[receiver].add(passed)
    items = jnp.searchsorted(jnp.cumsum(tallies), jnp.arange(rows * top), side="right").astype(jnp.int32)
    table = items.reshape(top, rows).T
    table = table[jax.random.permutation(jax.random.fold_in(own, 1), rows)]
    turn = jax.random.randint(jax.random.fold_in(own, 2), (rows, 1), 0, top)
    return jnp.take_along_axis(table, (jnp.arange(top)[None, :] + turn) % top, axis=1)


def portions_of(count, total, limit, slope, full):
    loads = [(1 << 20) // math.isqrt(rank ** slope) + 1 for rank in range(1, count + 1)]
    largest = limit if full else min(limit, max(-(-total // count), total * loads[0] // sum(loads)))
    least = 1 if total - largest >= count - 1 else 0
    holding, surplus = [largest] + [least] * (count - 1), total - largest - least * (count - 1)
    while surplus > 0:
        movable = [i for i in range(1, count) if holding[i] < largest] or [i for i in range(1, count) if holding[i] < limit]
        pool, budget = sum([loads[i] for i in movable]), surplus
        for i in movable:
            more = min(limit - holding[i], max(1, budget * loads[i] // pool), surplus)
            holding[i] = holding[i] + more
            surplus = surplus - more
    return np.array(holding)


def gaussian(own_key, extent, deviation, bound, shards=(), held_as=jnp.bfloat16):
    result = jax.random.normal(own_key, extent, jnp.float32) * deviation
    if len(shards) > 0:
        result = shard_levels(own_key, extent, shards, -0.22, 0.18) * result
    return jnp.clip(result, min=-bound, max=bound).astype(held_as)


def setup_inputs(seed: int = 0) -> dict:
    key_list = jax.random.split(jax.random.key(seed), 10)
    states = gaussian(key_list[0], (STEPS, H, ROWS), 1.0, 6.0, ((1, 16), (2, 8)))
    gate_inputs = gaussian(key_list[1], (STEPS, 3, H, ROWS), 1.0, 6.0, ((2, 16), (3, 8)))
    actions = jnp.clip(jax.random.uniform(key_list[2], (STEPS, A, ROWS), jnp.float32, -0.8984375, 0.8984375) * shard_levels(key_list[2], (STEPS, A, ROWS), ((2, 8),), -0.4, 0.0), -0.8984375, 0.8984375).astype(jnp.bfloat16)
    final_grad = gaussian(key_list[3], (H, ROWS), 1.0, 6.0, ((0, 16), (1, 8)))
    recur_weight = gaussian(key_list[4], (H, 3, H), H ** -0.5, 0.09375, ((2, 16),))
    act_weight = gaussian(key_list[5], (A, 3, H), A ** -0.5, 0.5, ((2, 16),))
    opp_first = gaussian(key_list[6], (MEMBERS, HID, H), H ** -0.5, 0.09375, ((0, 8), (2, 16)))
    opp_second = gaussian(key_list[7], (MEMBERS, A, HID), HID ** -0.5, 0.09375, ((0, 8),))
    opponent_keys = jax.random.split(jax.random.fold_in(key_list[8], 1), ROWS // R_DEV)
    opponent_turns = jax.random.permutation(jax.random.fold_in(key_list[8], 3), ROWS // R_DEV)
    opponent = jax.vmap(lambda own, number: assign_block(jax.random.fold_in(key_list[8], 2), own, number, R_DEV, MEMBERS, 1, CAP, 2))(opponent_keys, opponent_turns).reshape((ROWS, 1))
    return dict(states=states, gate_inputs=gate_inputs, actions=actions, final_grad=final_grad, recur_weight=recur_weight, act_weight=act_weight, opp_first=opp_first, opp_second=opp_second, opponent=opponent)


def gru_backward(gradient, pre_gates, latent):
    reset = jax.nn.sigmoid(pre_gates[0].astype(jnp.float32))
    cand_input = pre_gates[1].astype(jnp.float32)
    update = jax.nn.sigmoid(pre_gates[2].astype(jnp.float32) - 1.0)
    candidate = jnp.tanh(reset * cand_input)
    grad_cand = gradient * update * (1.0 - candidate * candidate)
    grad_reset = grad_cand * cand_input * reset * (1.0 - reset)
    grad_input = grad_cand * reset
    grad_update = gradient * (candidate - latent.astype(jnp.float32)) * update * (1.0 - update)
    direct = gradient * (1.0 - update)
    return direct, jnp.stack([grad_reset, grad_input, grad_update]).astype(jnp.bfloat16)


def silu_slope(values):
    logistic = jax.nn.sigmoid(values)
    return logistic * (1.0 + values * (1.0 - logistic))


def slot_table(opponent):
    chosen = opponent[:, 0].astype(jnp.int32)
    onehot = (chosen[:, None] == jnp.arange(MEMBERS, dtype=jnp.int32)[None, :]).astype(jnp.int32)
    blocks = onehot.reshape(N_POP, R_DEV, MEMBERS)
    position = jnp.sum((jnp.cumsum(blocks, axis=1) - blocks) * blocks, axis=2).reshape(ROWS).astype(jnp.int32)
    block_index = jnp.arange(ROWS, dtype=jnp.int32) // R_DEV
    slot_key = chosen * (N_POP * CAP) + block_index * CAP + position
    table = jnp.full((MEMBERS * N_POP * CAP,), -1, jnp.int32).at[slot_key].set(jnp.arange(ROWS, dtype=jnp.int32))
    return table.reshape(MEMBERS, N_POP * CAP)


def reference(states, gate_inputs, actions, final_grad, recur_weight, act_weight, opp_first, opp_second, opponent):
    table = slot_table(opponent)
    valid = table >= 0
    safe_rows = jnp.maximum(table, 0).astype(jnp.int32)
    share = H // N_UNIT
    slot_count = N_POP * CAP
    weight_units = jnp.moveaxis(recur_weight.reshape(H, 3, N_UNIT, share), 2, 0).reshape(N_UNIT, H, 3 * share)
    first_units = opp_first.reshape(MEMBERS, HID, N_UNIT, share)
    action_flat = act_weight.reshape(A, 3 * H)
    gradient = final_grad.astype(jnp.float32)
    weight_grad = jnp.zeros((A, 3 * H), jnp.float32)
    for step in reversed(range(STEPS)):
        latent = states[step]
        direct, pre_grads = gru_backward(gradient, gate_inputs[step], latent)
        grad_units = jnp.moveaxis(pre_grads.reshape(3, N_UNIT, share, ROWS), 1, 0).reshape(N_UNIT, 3 * share, ROWS)

        def add_unit(running, operands):
            partial_sum = jnp.dot(operands[0], operands[1], preferred_element_type=jnp.float32)
            rounded = lax.optimization_barrier(partial_sum.astype(jnp.bfloat16))
            return running + rounded.astype(jnp.float32), None

        carried, ignored = lax.scan(add_unit, jnp.zeros((H, ROWS), jnp.float32), (weight_units, grad_units))
        flat_grads = pre_grads.reshape(3 * H, ROWS)
        action_grad = jnp.dot(action_flat, flat_grads, preferred_element_type=jnp.float32)
        weight_grad = weight_grad + jnp.dot(actions[step], flat_grads.T, preferred_element_type=jnp.float32)
        taken = actions[step].astype(jnp.float32)
        policy_grad = (action_grad * (1.0 - taken * taken)).astype(jnp.bfloat16)

        def member_back(operands):
            first, second, rows_here, mask = operands
            latent_in = jnp.where(mask[None, :], jnp.take(latent, rows_here, axis=1), 0).astype(jnp.bfloat16)
            grad_in = jnp.where(mask[None, :], jnp.take(policy_grad, rows_here, axis=1), 0).astype(jnp.bfloat16)
            parts = jnp.einsum("kus,usn->ukn", first.astype(jnp.float32), latent_in.reshape(N_UNIT, share, slot_count).astype(jnp.float32), precision=lax.Precision.HIGHEST)
            rounded = lax.optimization_barrier(parts.astype(jnp.bfloat16)).astype(jnp.float32)
            summed = jnp.sum(rounded, axis=0)
            upward = jnp.dot(second.T, grad_in, preferred_element_type=jnp.float32)
            scaled = (upward * silu_slope(summed)).astype(jnp.bfloat16)
            return jnp.dot(first.reshape(HID, H).T, scaled, preferred_element_type=jnp.float32).astype(jnp.bfloat16)

        backs = lax.map(member_back, (first_units, opp_second, safe_rows, valid))
        contrib = jnp.where(valid[:, None, :], backs.astype(jnp.float32), 0.0)
        spread = jnp.moveaxis(contrib, 1, 0).reshape(H, MEMBERS * slot_count)
        from_opponent = jnp.zeros((H, ROWS), jnp.float32).at[:, safe_rows.reshape(-1)].add(spread)
        gradient = direct + carried + from_opponent
    return gradient.astype(jnp.bfloat16), weight_grad.reshape(A, 3, H)
```

```python
import functools
import types

import jax
import jax.numpy as jnp
from jax import lax
from jax.experimental import pallas as pl
from jax.experimental.pallas import tpu as pltpu
from jax.sharding import PartitionSpec as P

MESH = pl.DeviceIdType.MESH
F32 = jnp.float32
BF16 = jnp.bfloat16
PAIR = 48
RING = 4


def mm(a, b):
    return jnp.dot(a, b, preferred_element_type=F32)


def mm_nt(a, b):
    return lax.dot_general(a, b, (((1,), (1,)), ((), ())), preferred_element_type=F32)


def silu_slope(values):
    logistic = jax.nn.sigmoid(values)
    return logistic * (1.0 + values * (1.0 - logistic))


class Wire:
    def __init__(self, send_sems, recv_sems):
        self.send_sems = send_sems
        self.recv_sems = recv_sems
        self.count = 0

    def send(self, source, target, device):
        number = self.count
        self.count += 1
        copy = pltpu.make_async_remote_copy(
            src_ref=source,
            dst_ref=target,
            send_sem=self.send_sems.at[number],
            recv_sem=self.recv_sems.at[number],
            device_id=device,
            device_id_type=MESH,
        )
        copy.start()
        return copy, number, device

    def arrived(self, sent, landing):
        pltpu.make_async_remote_copy(
            src_ref=landing,
            dst_ref=landing,
            send_sem=self.send_sems.at[sent[1]],
            recv_sem=self.recv_sems.at[sent[1]],
            device_id=sent[2],
            device_id_type=MESH,
        ).wait_recv()


def wait_sends(sent):
    for entry in sent:
        entry[0].wait_send()


class Scatter:
    def __init__(self, wire, held, lo, hi, first, second, one, two, three, four, rest):
        self.wire, self.held, self.lo, self.hi = wire, held, lo, hi
        self.first, self.second = first, second
        self.one, self.two, self.three, self.four, self.rest = one, two, three, four, rest
        self.width = hi - lo

    def part(self, index, a, b):
        return self.held.at[index, a:b, :, self.lo : self.hi]

    def line(self, index, a, b):
        return self.rest.at[index, a:b, 0 : self.width]

    def stage1(self):
        w, (me, plus, minus) = self.wire, self.first
        up, down, far = (me + 1) % RING, (me + 3) % RING, (me + 2) % RING
        self.s1 = [
            w.send(self.part(far, 0, 2), self.one.at[0], plus),
            w.send(self.part(far, 2, 4), self.one.at[1], minus),
            w.send(self.part(up, 2, 4), self.two.at[0, 2:4], plus),
            w.send(self.part(down, 0, 2), self.two.at[1, 0:2], minus),
        ]

    def stage2(self):
        w, (me, plus, minus) = self.wire, self.first
        up, down = (me + 1) % RING, (me + 3) % RING
        lo, hi = self.lo, self.hi
        self.s2 = []
        for side, block, base, device in ((0, up, 0, plus), (1, down, 2, minus)):
            w.arrived(self.s1[side], self.one.at[side])

            def add(i, carry, side=side, block=block, base=base):
                total = self.held[block, base + i, :, lo:hi].astype(F32)
                total = total + self.one[side, i].astype(F32)
                self.held[block, base + i, :, lo:hi] = total.astype(BF16)
                return carry

            lax.fori_loop(0, 2, add, 0)
            self.s2.append(
                w.send(
                    self.part(block, base, base + 2), self.two.at[side, base : base + 2], device
                )
            )

    def stage3(self):
        w, me = self.wire, self.first[0]
        at, plus, minus = self.second
        lo, hi = self.lo, self.hi
        w.arrived(self.s1[2], self.two.at[0, 2:4])
        w.arrived(self.s1[3], self.two.at[1, 0:2])
        w.arrived(self.s2[0], self.two.at[0, 0:2])
        w.arrived(self.s2[1], self.two.at[1, 2:4])

        def add(i, carry):
            total = self.held[me, i, :, lo:hi].astype(F32) + self.two[0, i].astype(F32)
            total = total + self.two[1, i].astype(F32)
            self.rest[i, :, 0 : self.width] = total.astype(BF16)
            return carry

        lax.fori_loop(0, RING, add, 0)
        up, down, far = (at + 1) % RING, (at + 3) % RING, (at + 2) % RING
        self.s3 = [
            w.send(self.line(far, 0, 64), self.three.at[0], plus),
            w.send(self.line(far, 64, 128), self.three.at[1], minus),
            w.send(self.line(up, 64, 128), self.four.at[0, 64:128], plus),
            w.send(self.line(down, 0, 64), self.four.at[1, 0:64], minus),
        ]

    def stage4(self):
        w = self.wire
        at, plus, minus = self.second
        up, down = (at + 1) % RING, (at + 3) % RING
        self.s4 = []
        for side, block, base, device in ((0, up, 0, plus), (1, down, 64, minus)):
            w.arrived(self.s3[side], self.three.at[side])
            total = self.rest[block, base : base + 64, 0 : self.width].astype(F32)
            total = total + self.three[side].astype(F32)
            self.rest[block, base : base + 64, 0 : self.width] = total.astype(BF16)
            self.s4.append(
                w.send(
                    self.line(block, base, base + 64), self.four.at[side, base : base + 64], device
                )
            )

    def landed(self):
        w = self.wire
        w.arrived(self.s3[2], self.four.at[0, 64:128])
        w.arrived(self.s3[3], self.four.at[1, 0:64])
        w.arrived(self.s4[0], self.four.at[0, 0:64])
        w.arrived(self.s4[1], self.four.at[1, 64:128])
        wait_sends(self.s1 + self.s2 + self.s3 + self.s4)

    def result(self, a, b):
        total = self.rest[self.second[0], :, a:b].astype(F32) + self.four[0, :, a:b].astype(F32)
        return total + self.four[1, :, a:b].astype(F32)


class Gather:
    def __init__(self, wire, held, rows, first, second):
        self.wire, self.held, self.rows = wire, held, rows
        self.first, self.second = first, second

    def stage1(self):
        f, (at, plus, minus) = self.first[0], self.second
        own = self.held.at[f, at]
        self.a1 = [self.wire.send(own, own, plus), self.wire.send(own, own, minus)]

    def stage2(self):
        f, (at, plus, minus) = self.first[0], self.second
        half = self.rows // 2
        below, above = (at + 3) % RING, (at + 1) % RING
        self.wire.arrived(self.a1[0], self.held.at[f, below])
        low = self.held.at[f, below, 0:half]
        first = self.wire.send(low, low, plus)
        self.wire.arrived(self.a1[1], self.held.at[f, above])
        high = self.held.at[f, above, half : 2 * half]
        self.a2 = [first, self.wire.send(high, high, minus)]

    def stage3(self):
        f, plus, minus = self.first
        at = self.second[0]
        half = self.rows // 2
        far = (at + 2) % RING
        self.wire.arrived(self.a2[0], self.held.at[f, far, 0:half])
        self.wire.arrived(self.a2[1], self.held.at[f, far, half : 2 * half])
        line = self.held.at[f]
        self.a3 = [self.wire.send(line, line, plus), self.wire.send(line, line, minus)]

    def stage4(self):
        f, plus, minus = self.first
        below, above = (f + 3) % RING, (f + 1) % RING
        self.wire.arrived(self.a3[0], self.held.at[below])
        low = self.held.at[below, 0:2]
        first = self.wire.send(low, low, plus)
        self.wire.arrived(self.a3[1], self.held.at[above])
        high = self.held.at[above, 2:4]
        self.a4 = [first, self.wire.send(high, high, minus)]

    def landed(self):
        far = (self.first[0] + 2) % RING
        self.wire.arrived(self.a4[0], self.held.at[far, 0:2])
        self.wire.arrived(self.a4[1], self.held.at[far, 2:4])
        wait_sends(self.a1 + self.a2 + self.a3 + self.a4)


def kernel(
    steps,
    cap,
    groups,
    members,
    blocks,
    states,
    gates,
    actions,
    final_grad,
    act_w,
    opp_row,
    opp_col,
    recur_hbm,
    first_hbm,
    second_hbm,
    start_out,
    weight_out,
    *scratch,
):
    shapes = scratch_shapes(steps, cap, groups, members, blocks)
    s = types.SimpleNamespace(**jax.tree.unflatten(jax.tree.structure(shapes), scratch))
    rows = 128
    half = cap // 2
    last = steps - 1
    pair_rows = groups * PAIR
    p = lax.axis_index("pop")
    u = lax.axis_index("unit")
    z, y = u // RING, u % RING

    def at_unit(zz, yy):
        return (p, (zz % RING) * RING + yy % RING)

    z_ring = (z, at_unit(z + 1, y), at_unit(z + 3, y))
    y_ring = (y, at_unit(z, y + 1), at_unit(z, y + 3))
    z_peers = [at_unit(z + k, y) for k in (1, 2, 3)]
    y_peers = [at_unit(z, y + k) for k in (1, 2, 3)]
    pop_peers = [((p + k) % groups, u) for k in range(1, groups)]
    barrier = pltpu.get_barrier_semaphore()
    for device in z_peers + y_peers + pop_peers:
        pl.semaphore_signal(barrier, inc=1, device_id=device, device_id_type=MESH)

    loads = [
        pltpu.make_async_copy(first_hbm, s.first, s.load_sems.at[0]),
        pltpu.make_async_copy(recur_hbm, s.recur, s.load_sems.at[1]),
        pltpu.make_async_copy(second_hbm, s.second, s.load_sems.at[2]),
    ]
    for load in loads:
        load.start()
    wire = Wire(s.send_sems, s.recv_sems)

    def keys(chosen, axis):
        shape = (8, rows) if axis == 1 else (rows, 8)
        group_of = (chosen // members).astype(F32)
        index = lax.broadcasted_iota(jnp.int32, shape, 1 - axis).astype(F32)
        onehot = jnp.where(group_of == index, 1.0, 0.0)
        a = lax.broadcasted_iota(jnp.int32, (rows, rows), 0)
        b = lax.broadcasted_iota(jnp.int32, (rows, rows), 1)
        if axis == 1:
            rank = mm(onehot.astype(BF16), jnp.where(a < b, 1.0, 0.0).astype(BF16))
        else:
            rank = mm(jnp.where(b < a, 1.0, 0.0).astype(BF16), onehot.astype(BF16))
        return jnp.sum(onehot * (rank + index * PAIR), axis=1 - axis, keepdims=True)

    key_row = keys(opp_row[...], 1)
    key_col = keys(opp_col[...], 0)
    slot = lax.broadcasted_iota(jnp.int32, (pair_rows, rows), 0).astype(F32)
    s.pack[...] = jnp.where(slot == key_row, 1.0, 0.0).astype(BF16)
    slot = lax.broadcasted_iota(jnp.int32, (rows, pair_rows), 1).astype(F32)
    s.unpack[...] = jnp.where(slot == key_col, 1.0, 0.0).astype(BF16)
    ident = (opp_col[...] % members + 1).astype(F32)
    ident = jnp.broadcast_to(ident, (rows, 128)).astype(BF16)
    ident = mm(s.pack[...], ident).astype(BF16)
    packed = mm_nt(s.pack[...], states[last]).astype(BF16)
    for g in range(groups):
        s.out_late[g, :, 0:256] = packed[g * PAIR : (g + 1) * PAIR]
        s.out_late[g, :, 256:384] = ident[g * PAIR : (g + 1) * PAIR]

    pl.semaphore_wait(barrier, len(z_peers + y_peers + pop_peers))

    def exchange(source, target):
        sent = [
            wire.send(source.at[(p + k) % groups], target.at[p], device)
            for k, device in zip(range(1, groups), pop_peers)
        ]
        target[p] = source[p]
        return sent

    def exchanged(sent, target):
        for k, entry in zip(range(1, groups), sent):
            wire.arrived(entry, target.at[(p + groups - k) % groups])

    late = exchange(s.out_late, s.in_late)
    for t in range(last):
        packed = mm_nt(s.pack[...], states[t]).astype(BF16)
        for g in range(groups):
            s.out_early[g, t] = packed[g * PAIR : (g + 1) * PAIR]
    early = exchange(s.out_early, s.in_early)

    def factors(t):
        reset = jax.nn.sigmoid(gates[t, 0].astype(F32))
        cand_in = gates[t, 1].astype(F32)
        update = jax.nn.sigmoid(gates[t, 2].astype(F32) - 1.0)
        candidate = jnp.tanh(reset * cand_in)
        e = update * (1.0 - candidate * candidate)
        rest = 1.0 - update
        s.factor[t, 0] = e * cand_in * reset * (1.0 - reset)
        s.factor[t, 1] = e * reset
        s.factor[t, 2] = (candidate - states[t].astype(F32)) * update * rest
        s.factor[t, 3] = rest
        taken = actions[t].astype(F32)
        s.bound[t] = 1.0 - taken * taken

    factors(last)
    s.grad[...] = final_grad[...].astype(F32)

    def begin(t):
        for q in range(3):
            s.pre[q] = (s.grad[...] * s.factor[t, q]).astype(BF16)
        part = mm(act_w[0], s.pre[0]) + mm(act_w[1], s.pre[1]) + mm(act_w[2], s.pre[2])
        s.act_own[t, 0] = part.astype(BF16)
        return [
            wire.send(s.act_own.at[t, 0], s.act_in.at[t, 0, i], device)
            for i, device in enumerate(z_peers)
        ]

    def act_sum(t, stage, sent):
        for i, entry in enumerate(sent):
            wire.arrived(entry, s.act_in.at[t, stage, i])
        total = s.act_own[t, stage].astype(F32) + s.act_in[t, stage, 0].astype(F32)
        total = total + s.act_in[t, stage, 1].astype(F32)
        return total + s.act_in[t, stage, 2].astype(F32)

    def act_second(t, sent):
        s.act_own[t, 1] = act_sum(t, 0, sent).astype(BF16)
        return [
            wire.send(s.act_own.at[t, 1], s.act_in.at[t, 1, i], device)
            for i, device in enumerate(y_peers)
        ]

    def dispatch(t, sent):
        policy = (act_sum(t, 1, sent) * s.bound[t]).astype(BF16)
        packed = mm_nt(s.pack[...], policy).astype(BF16)
        for g in range(groups):
            s.policy_out[t, g] = packed[g * PAIR : (g + 1) * PAIR]
        return exchange(s.policy_out.at[t], s.policy_in.at[t])

    def collect(t, sent):
        exchanged(sent, s.policy_in.at[t])
        arrived = s.policy_in[t].reshape(pair_rows, 128)
        policy = mm(s.choose[...], arrived).astype(BF16)
        for m in range(members):
            s.policy[:, m * 128 : (m + 1) * 128] = policy * s.mask[m, :, 0:128]

    def store_blocks(b, total, lo):
        hi = lo + total.shape[1]
        s.held_a[b // RING, b % RING, :, lo:hi] = total[0:128]
        s.held_b[b % RING, b // RING, :, lo:hi] = total[128:256]

    def carried_part():
        def two(i, carry):
            at = pl.ds(pl.multiple_of(i * 512, 512), 512)
            total = mm(s.recur[0, at, :], s.pre[0]) + mm(s.recur[1, at, :], s.pre[1])
            total = (total + mm(s.recur[2, at, :], s.pre[2])).astype(BF16)
            store_blocks(2 * i, total[0:256], 0)
            store_blocks(2 * i + 1, total[256:512], 0)
            return carry

        lax.fori_loop(0, blocks // 2, two, 0)

    def weight_part(t, start):
        for q in range(3):
            share = mm_nt(actions[t], s.pre[q])
            at = slice(q * 256, (q + 1) * 256)
            if start:
                s.weight[:, at] = share
            else:
                s.weight[:, at] += share

    def latents(t):
        if t == last:
            arrived = s.in_late[:, :, 0:256].reshape(pair_rows, 256)
        else:
            arrived = s.in_early[:, t].reshape(pair_rows, 256)
        chosen = mm(s.choose[...], arrived).T
        for m in range(members):
            s.latent[m] = jnp.where(s.names[0:1] == m + 1, chosen, 0.0).astype(BF16)

    def hidden_part(t):
        latents(t)

        def two(i, carry):
            at = pl.ds(pl.multiple_of(i * 512, 512), 512)
            total = mm(s.first[0, at, :], s.latent[0])
            for m in range(1, members):
                total = total + mm(s.first[m, at, :], s.latent[m])
            total = total.astype(BF16)
            store_blocks(2 * i, total[0:256], 128)
            store_blocks(2 * i + 1, total[256:512], 128)
            return carry

        lax.fori_loop(0, blocks // 2, two, 0)

    def scatters(which, lo, hi):
        one, two = s.sums[which]
        return [
            Scatter(wire, s.held_a, lo, hi, z_ring, y_ring, *one, s.rest_a),
            Scatter(wire, s.held_b, lo, hi, y_ring, z_ring, *two, s.rest_b),
        ]

    def slopes(t, pair, lo):
        hidden = jnp.concatenate([one.result(lo, lo + cap) for one in pair], axis=0)
        slope = silu_slope(hidden).T.astype(BF16)
        s.slope_a[t % 2, z, y] = slope[0:half]
        s.slope_b[t % 2, y, z] = slope[half:cap]
        made = [
            Gather(wire, s.slope_a.at[t % 2], half, z_ring, y_ring),
            Gather(wire, s.slope_b.at[t % 2], half, y_ring, z_ring),
        ]
        for one in made:
            one.stage1()
        return made

    def backward(t):
        def one(b, carry):
            at = pl.ds(pl.multiple_of(b * 256, 256), 256)
            upward = mm(s.policy[:, 0:128], s.second[0, :, at])
            for m in range(1, members):
                upward = upward + mm(s.policy[:, m * 128 : (m + 1) * 128], s.second[m, :, at])
            low = upward[0:half] * s.slope_a[t % 2, b // RING, b % RING].astype(F32)
            high = upward[half:cap] * s.slope_b[t % 2, b % RING, b // RING].astype(F32)
            s.scaled[0:half, at] = low.astype(BF16)
            s.scaled[half:cap, at] = high.astype(BF16)
            return carry

        lax.fori_loop(0, blocks, one, 0)
        s.back[...] = jnp.zeros_like(s.back)

        def member(m, carry):
            s.back[...] += s.mask[m].astype(F32) * mm(s.scaled[...], s.first[m])
            return carry

        lax.fori_loop(0, members, member, 0)
        packed = mm(s.spread[...], s.back[...].astype(BF16)).astype(BF16)
        for g in range(groups):
            s.return_out[t, g] = packed[g * PAIR : (g + 1) * PAIR]
        return exchange(s.return_out.at[t], s.return_in.at[t])

    def finish(t, sent, pair):
        exchanged(sent, s.return_in.at[t])
        own = mm(s.unpack[...], s.return_in[t].reshape(pair_rows, 256)).T
        direct = s.grad[...] * s.factor[t, 3]
        s.grad[0:128] = direct[0:128] + pair[0].result(0, 128) + own[0:128]
        s.grad[128:256] = direct[128:256] + pair[1].result(0, 128) + own[128:256]

    sends = []
    act = begin(last)

    exchanged(late, s.in_late)
    names_in = s.in_late[:, :, 256:384].reshape(pair_rows, 128)
    lane = lax.broadcasted_iota(jnp.int32, (8, 128), 1)
    picker = jnp.where(lane == 0, 1.0, 0.0).astype(BF16)
    names_row = mm_nt(picker, names_in)
    held_row = jnp.where(names_row > 0.5, 1.0, 0.0)
    a = lax.broadcasted_iota(jnp.int32, (pair_rows, pair_rows), 0)
    b = lax.broadcasted_iota(jnp.int32, (pair_rows, pair_rows), 1)
    place_row = mm(held_row.astype(BF16), jnp.where(a < b, 1.0, 0.0).astype(BF16))
    spot = lax.broadcasted_iota(jnp.int32, (cap, pair_rows), 0).astype(F32)
    chosen = jnp.where(spot == place_row[0:1], held_row[0:1], 0.0).astype(BF16)
    s.choose[...] = chosen
    held_col = jnp.where(names_in.astype(F32) > 0.5, 1.0, 0.0)
    place_col = mm(jnp.where(b < a, 1.0, 0.0).astype(BF16), held_col.astype(BF16))
    spot = lax.broadcasted_iota(jnp.int32, (pair_rows, cap), 1).astype(F32)
    chosen_t = jnp.where(spot == place_col[:, 0:1], held_col[:, 0:1], 0.0)
    s.spread[...] = chosen_t.astype(BF16)
    s.names[...] = mm(names_row.astype(BF16), s.spread[...])
    slot_name = mm(s.choose[...], names_in)
    for m in range(members):
        mask = jnp.where(jnp.abs(slot_name[:, 0:1] - (m + 1)) < 0.5, 1.0, 0.0)
        s.mask[m] = jnp.broadcast_to(mask, (cap, 256)).astype(BF16)

    loads[0].wait()
    hidden_part(last)
    opening = scatters(steps, 128, 128 + cap)
    for one in opening:
        one.stage1()
    act2 = act_second(last, act)
    loads[1].wait()
    carried_part()
    for one in opening:
        one.stage2()
    sends += act + act2
    out = dispatch(last, act2)
    weight_part(last, True)
    for one in opening:
        one.stage3()
    for t in range(last):
        factors(t)
    exchanged(early, s.in_early)
    for one in opening:
        one.stage4()
    loads[2].wait()
    collect(last, out)
    for one in opening:
        one.landed()
    gather = slopes(last, opening, 0)
    hidden_part(last - 1)
    pair = scatters(last, 0, 128 + cap)
    for one in pair:
        one.stage1()
    for one in gather:
        one.stage2()
    for one in pair:
        one.stage2()
    for one in gather:
        one.stage3()
    for one in pair:
        one.stage3()
    for one in gather:
        one.stage4()
    for one in pair:
        one.stage4()
    for one in gather:
        one.landed()
    sends += late + early + out

    for t in range(last, -1, -1):
        if t < last:
            act = begin(t)
            if t > 0:
                pair = scatters(t, 0, 128 + cap)
            else:
                pair = scatters(t, 0, 128)
            carried_part()
            for one in pair:
                one.stage1()
            for one in gather:
                one.stage3()
            act2 = act_second(t, act)
            weight_part(t, False)
            for one in pair:
                one.stage2()
            for one in gather:
                one.stage4()
            if t == 0:
                pieces = [
                    s.weight[k * 16 : (k + 1) * 16].astype(BF16) for k in range(groups)
                ]
                for k in range(groups):
                    s.share_out[k] = pieces[k]
                shares = exchange(s.share_out, s.share_in)
            out = dispatch(t, act2)
            for one in pair:
                one.stage3()
            sends += act + act2 + out
            collect(t, out)
            for one in pair:
                one.stage4()
            if t == 0:
                exchanged(shares, s.share_in)
                total = s.share_in[0].astype(F32)
                for k in range(1, groups):
                    total = total + s.share_in[k].astype(F32)
                s.share_all[p] = total.astype(BF16)
                whole = [
                    wire.send(s.share_all.at[p], s.share_all.at[p], device)
                    for device in pop_peers
                ]
                sends += shares + whole
            for one in gather:
                one.landed()
        back = backward(t)
        sends += back
        for one in pair:
            one.landed()
        if t > 0:
            gather = slopes(t - 1, pair, 128)
            if t > 1:
                hidden_part(t - 2)
            for one in gather:
                one.stage2()
        else:
            exchanged(whole, s.share_all)
            for k in range(groups):
                weight_out[k * 16 : (k + 1) * 16] = s.share_all[k].astype(F32)
        finish(t, back, pair)
    start_out[...] = s.grad[...].astype(BF16)
    wait_sends(sends)


def sum_bufs(width):
    def four():
        return (
            pltpu.VMEM((2, 2, 128, width), BF16),
            pltpu.VMEM((2, RING, 128, width), BF16),
            pltpu.VMEM((2, 64, width), BF16),
            pltpu.VMEM((2, 128, width), BF16),
        )

    return four(), four()


def scratch_shapes(steps, cap, groups, members, blocks):
    half = cap // 2
    v = pltpu.VMEM
    shapes = dict(
        first=v((members, blocks * 256, 256), BF16),
        recur=v((3, blocks * 256, 256), BF16),
        second=v((members, 128, blocks * 256), BF16),
        pack=v((groups * PAIR, 128), BF16),
        unpack=v((128, groups * PAIR), BF16),
        choose=v((cap, groups * PAIR), BF16),
        spread=v((groups * PAIR, cap), BF16),
        mask=v((members, cap, 256), BF16),
        out_late=v((groups, PAIR, 384), BF16),
        in_late=v((groups, PAIR, 384), BF16),
        out_early=v((groups, steps - 1, PAIR, 256), BF16),
        in_early=v((groups, steps - 1, PAIR, 256), BF16),
        factor=v((steps, 4, 256, 128), F32),
        bound=v((steps, 128, 128), F32),
        grad=v((256, 128), F32),
        pre=v((3, 256, 128), BF16),
        act_own=v((steps, 2, 128, 128), BF16),
        act_in=v((steps, 2, 3, 128, 128), BF16),
        policy_out=v((steps, groups, PAIR, 128), BF16),
        policy_in=v((steps, groups, PAIR, 128), BF16),
        policy=v((cap, members * 128), BF16),
        latent=v((members, 256, cap), BF16),
        names=v((8, cap), F32),
        scaled=v((cap, blocks * 256), BF16),
        weight=v((128, 768), F32),
        share_out=v((groups, 16, 768), BF16),
        share_in=v((groups, 16, 768), BF16),
        share_all=v((groups, 16, 768), BF16),
        back=v((cap, 256), F32),
        return_out=v((steps, groups, PAIR, 256), BF16),
        return_in=v((steps, groups, PAIR, 256), BF16),
        held_a=v((RING, RING, 128, 128 + cap), BF16),
        held_b=v((RING, RING, 128, 128 + cap), BF16),
        rest_a=v((RING, 128, 128 + cap), BF16),
        rest_b=v((RING, 128, 128 + cap), BF16),
        slope_a=v((2, RING, RING, half, 256), BF16),
        slope_b=v((2, RING, RING, half, 256), BF16),
    )
    shapes.update(sums=[sum_bufs(128 + cap if t > 0 else 128) for t in range(steps)] + [sum_bufs(cap)])
    copies = 4 * (groups - 1) + (steps + 1) * 24 + steps * (16 + 6 + 2 * (groups - 1))
    shapes.update(send_sems=pltpu.SemaphoreType.DMA((copies,)))
    shapes.update(recv_sems=pltpu.SemaphoreType.DMA((copies,)))
    shapes.update(load_sems=pltpu.SemaphoreType.DMA((3,)))
    return shapes


def call(cap, groups, blocks, name, collective_id):
    def run(states, gates, actions, final_grad, act_w, opp_row, opp_col, recur, first, second):
        steps, members = states.shape[0], first.shape[0]
        vmem = pl.BlockSpec(memory_space=pltpu.VMEM)
        hbm = pl.BlockSpec(memory_space=pl.ANY)
        return pl.pallas_call(
            functools.partial(kernel, steps, cap, groups, members, blocks),
            out_shape=(
                jax.ShapeDtypeStruct((256, 128), BF16),
                jax.ShapeDtypeStruct((128, 768), F32),
            ),
            in_specs=[vmem] * 7 + [hbm] * 3,
            out_specs=(vmem, vmem),
            scratch_shapes=jax.tree.leaves(scratch_shapes(steps, cap, groups, members, blocks)),
            compiler_params=pltpu.CompilerParams(
                collective_id=collective_id, has_side_effects=True, vmem_limit_bytes=62 << 20
            ),
            name=name,
        )(states, gates, actions, final_grad, act_w, opp_row, opp_col, recur, first, second)

    return run


def body(
    states,
    gate_inputs,
    actions,
    final_grad,
    recur_weight,
    act_weight,
    opp_first,
    opp_second,
    opponent,
):
    groups = lax.axis_size("pop")
    blocks = lax.axis_size("unit")
    cap = groups * PAIR
    recur = jnp.transpose(recur_weight, (1, 0, 2))
    act_w = jnp.transpose(act_weight, (1, 0, 2))
    start, weight = call(cap, groups, blocks, "steps_back", 0)(
        states,
        gate_inputs,
        actions,
        final_grad,
        act_w,
        opponent.reshape(1, -1),
        opponent,
        recur,
        opp_first,
        opp_second,
    )
    return start, weight.reshape(act_weight.shape)


def solution(mesh):
    placed = (
        P(None, "unit", "pop"),
        P(None, None, "unit", "pop"),
        P(None, None, "pop"),
        P("unit", "pop"),
        P(None, None, "unit"),
        P(None, None, "unit"),
        P("pop", None, "unit"),
        P("pop", None, None),
        P("pop", None),
    )
    return jax.shard_map(
        body,
        mesh=mesh,
        in_specs=placed,
        out_specs=(P("unit", "pop"), P(None, None, "unit")),
        check_vma=False,
    )
```

```python
import functools
import types

import jax
import jax.numpy as jnp
from jax import lax
from jax.experimental import pallas as pl
from jax.experimental.pallas import tpu as pltpu
from jax.sharding import PartitionSpec as P

MESH = pl.DeviceIdType.MESH
F32 = jnp.float32
BF16 = jnp.bfloat16
PAIR = 48
FEW = 256
RING = 4


def mm(a, b):
    return jnp.dot(a, b, preferred_element_type=F32)


def mm_nt(a, b):
    return lax.dot_general(a, b, (((1,), (1,)), ((), ())), preferred_element_type=F32)


def silu_slope(values):
    logistic = jax.nn.sigmoid(values)
    return logistic * (1.0 + values * (1.0 - logistic))


class Wire:
    def __init__(self, send_sems, recv_sems):
        self.send_sems = send_sems
        self.recv_sems = recv_sems
        self.count = 0

    def send(self, source, target, device):
        number = self.count
        self.count += 1
        copy = pltpu.make_async_remote_copy(
            src_ref=source,
            dst_ref=target,
            send_sem=self.send_sems.at[number],
            recv_sem=self.recv_sems.at[number],
            device_id=device,
            device_id_type=MESH,
        )
        copy.start()
        return copy, number, device

    def arrived(self, sent, landing):
        pltpu.make_async_remote_copy(
            src_ref=landing,
            dst_ref=landing,
            send_sem=self.send_sems.at[sent[1]],
            recv_sem=self.recv_sems.at[sent[1]],
            device_id=sent[2],
            device_id_type=MESH,
        ).wait_recv()


def wait_sends(sent):
    for entry in sent:
        entry[0].wait_send()


class Scatter:
    def __init__(self, wire, held, lo, hi, first, second, one, two, three, four, rest):
        self.wire, self.held, self.lo, self.hi = wire, held, lo, hi
        self.first, self.second = first, second
        self.one, self.two, self.three, self.four, self.rest = one, two, three, four, rest
        self.width = hi - lo

    def part(self, index, a, b):
        return self.held.at[index, a:b, :, self.lo : self.hi]

    def line(self, index, a, b):
        return self.rest.at[index, a:b, 0 : self.width]

    def stage0(self):
        w, (me, plus, minus) = self.wire, self.first
        far = (me + 2) % RING
        self.s0 = [
            w.send(self.part(far, 0, 2), self.one.at[0], plus),
            w.send(self.part(far, 2, 4), self.one.at[1], minus),
        ]

    def stage1(self):
        w, (me, plus, minus) = self.wire, self.first
        up, down = (me + 1) % RING, (me + 3) % RING
        self.s1 = [
            w.send(self.part(up, 2, 4), self.two.at[0, 2:4], plus),
            w.send(self.part(down, 0, 2), self.two.at[1, 0:2], minus),
        ]

    def stage2(self):
        w, (me, plus, minus) = self.wire, self.first
        up, down = (me + 1) % RING, (me + 3) % RING
        lo, hi = self.lo, self.hi
        self.s2 = []
        for side, block, base, device in ((0, up, 0, plus), (1, down, 2, minus)):
            w.arrived(self.s0[side], self.one.at[side])

            def add(i, carry, side=side, block=block, base=base):
                total = self.held[block, base + i, :, lo:hi].astype(F32)
                total = total + self.one[side, i].astype(F32)
                self.held[block, base + i, :, lo:hi] = total.astype(BF16)
                return carry

            lax.fori_loop(0, 2, add, 0)
            self.s2.append(
                w.send(
                    self.part(block, base, base + 2), self.two.at[side, base : base + 2], device
                )
            )

    def stage3(self):
        w, me = self.wire, self.first[0]
        at, plus, minus = self.second
        lo, hi = self.lo, self.hi
        w.arrived(self.s1[0], self.two.at[0, 2:4])
        w.arrived(self.s1[1], self.two.at[1, 0:2])
        w.arrived(self.s2[0], self.two.at[0, 0:2])
        w.arrived(self.s2[1], self.two.at[1, 2:4])

        def add(i, carry):
            total = self.held[me, i, :, lo:hi].astype(F32) + self.two[0, i].astype(F32)
            total = total + self.two[1, i].astype(F32)
            self.rest[i, :, 0 : self.width] = total.astype(BF16)
            return carry

        lax.fori_loop(0, RING, add, 0)
        up, down, far = (at + 1) % RING, (at + 3) % RING, (at + 2) % RING
        self.s3 = [
            w.send(self.line(far, 0, 64), self.three.at[0], plus),
            w.send(self.line(far, 64, 128), self.three.at[1], minus),
            w.send(self.line(up, 64, 128), self.four.at[0, 64:128], plus),
            w.send(self.line(down, 0, 64), self.four.at[1, 0:64], minus),
        ]

    def stage4(self):
        w = self.wire
        at, plus, minus = self.second
        up, down = (at + 1) % RING, (at + 3) % RING
        self.s4 = []
        for side, block, base, device in ((0, up, 0, plus), (1, down, 64, minus)):
            w.arrived(self.s3[side], self.three.at[side])
            total = self.rest[block, base : base + 64, 0 : self.width].astype(F32)
            total = total + self.three[side].astype(F32)
            self.rest[block, base : base + 64, 0 : self.width] = total.astype(BF16)
            self.s4.append(
                w.send(
                    self.line(block, base, base + 64), self.four.at[side, base : base + 64], device
                )
            )

    def landed(self):
        w = self.wire
        w.arrived(self.s3[2], self.four.at[0, 64:128])
        w.arrived(self.s3[3], self.four.at[1, 0:64])
        w.arrived(self.s4[0], self.four.at[0, 0:64])
        w.arrived(self.s4[1], self.four.at[1, 64:128])
        wait_sends(self.s0 + self.s1 + self.s2 + self.s3 + self.s4)

    def result(self, a, b):
        total = self.rest[self.second[0], :, a:b].astype(F32) + self.four[0, :, a:b].astype(F32)
        return total + self.four[1, :, a:b].astype(F32)


class Gather:
    def __init__(self, wire, held, rows, first, second):
        self.wire, self.held, self.rows = wire, held, rows
        self.first, self.second = first, second

    def stage1(self):
        f, (at, plus, minus) = self.first[0], self.second
        own = self.held.at[f, at]
        self.a1 = [self.wire.send(own, own, plus), self.wire.send(own, own, minus)]

    def stage2(self):
        f, (at, plus, minus) = self.first[0], self.second
        half = self.rows // 2
        below, above = (at + 3) % RING, (at + 1) % RING
        self.wire.arrived(self.a1[0], self.held.at[f, below])
        low = self.held.at[f, below, 0:half]
        first = self.wire.send(low, low, plus)
        self.wire.arrived(self.a1[1], self.held.at[f, above])
        high = self.held.at[f, above, half : 2 * half]
        self.a2 = [first, self.wire.send(high, high, minus)]

    def stage3(self):
        f, plus, minus = self.first
        at = self.second[0]
        half = self.rows // 2
        far = (at + 2) % RING
        self.wire.arrived(self.a2[0], self.held.at[f, far, 0:half])
        self.wire.arrived(self.a2[1], self.held.at[f, far, half : 2 * half])
        line = self.held.at[f]
        self.a3 = [self.wire.send(line, line, plus), self.wire.send(line, line, minus)]

    def stage4(self):
        f, plus, minus = self.first
        below, above = (f + 3) % RING, (f + 1) % RING
        self.wire.arrived(self.a3[0], self.held.at[below])
        low = self.held.at[below, 0:2]
        first = self.wire.send(low, low, plus)
        self.wire.arrived(self.a3[1], self.held.at[above])
        high = self.held.at[above, 2:4]
        self.a4 = [first, self.wire.send(high, high, minus)]

    def landed(self):
        far = (self.first[0] + 2) % RING
        self.wire.arrived(self.a4[0], self.held.at[far, 0:2])
        self.wire.arrived(self.a4[1], self.held.at[far, 2:4])
        wait_sends(self.a1 + self.a2 + self.a3 + self.a4)


def kernel(
    steps,
    cap,
    deep,
    groups,
    members,
    blocks,
    states,
    gates,
    actions,
    final_grad,
    act_w,
    opp_row,
    opp_col,
    recur_hbm,
    first_hbm,
    second_hbm,
    start_out,
    weight_out,
    *scratch,
):
    shapes = scratch_shapes(steps, cap, deep, groups, members, blocks)
    s = types.SimpleNamespace(**jax.tree.unflatten(jax.tree.structure(shapes), scratch))
    rows = 128
    half = cap // 2
    last = steps - 1
    pair_rows = groups * PAIR
    p = lax.axis_index("pop")
    u = lax.axis_index("unit")
    z, y = u // RING, u % RING

    def at_unit(zz, yy):
        return (p, (zz % RING) * RING + yy % RING)

    z_ring = (z, at_unit(z + 1, y), at_unit(z + 3, y))
    y_ring = (y, at_unit(z, y + 1), at_unit(z, y + 3))
    z_peers = [at_unit(z + k, y) for k in (1, 2, 3)]
    y_peers = [at_unit(z, y + k) for k in (1, 2, 3)]
    pop_peers = [((p + k) % groups, u) for k in range(1, groups)]
    barrier = pltpu.get_barrier_semaphore()
    for device in z_peers + y_peers + pop_peers:
        pl.semaphore_signal(barrier, inc=1, device_id=device, device_id_type=MESH)

    loads = [
        pltpu.make_async_copy(first_hbm, s.first, s.load_sems.at[0]),
        pltpu.make_async_copy(recur_hbm, s.recur, s.load_sems.at[1]),
        pltpu.make_async_copy(second_hbm, s.second, s.load_sems.at[2]),
    ]
    for load in loads:
        load.start()
    wire = Wire(s.send_sems, s.recv_sems)

    def keys(chosen, axis):
        shape = (8, rows) if axis == 1 else (rows, 8)
        group_of = (chosen // members).astype(F32)
        index = lax.broadcasted_iota(jnp.int32, shape, 1 - axis).astype(F32)
        onehot = jnp.where(group_of == index, 1.0, 0.0)
        a = lax.broadcasted_iota(jnp.int32, (rows, rows), 0)
        b = lax.broadcasted_iota(jnp.int32, (rows, rows), 1)
        if axis == 1:
            rank = mm(onehot.astype(BF16), jnp.where(a < b, 1.0, 0.0).astype(BF16))
        else:
            rank = mm(jnp.where(b < a, 1.0, 0.0).astype(BF16), onehot.astype(BF16))
        return jnp.sum(onehot * (rank + index * PAIR), axis=1 - axis, keepdims=True)

    key_row = keys(opp_row[...], 1)
    key_col = keys(opp_col[...], 0)
    slot = lax.broadcasted_iota(jnp.int32, (pair_rows, rows), 0).astype(F32)
    s.pack[...] = jnp.where(slot == key_row, 1.0, 0.0).astype(BF16)
    slot = lax.broadcasted_iota(jnp.int32, (rows, pair_rows), 1).astype(F32)
    s.unpack[...] = jnp.where(slot == key_col, 1.0, 0.0).astype(BF16)
    ident = (opp_col[...] % members + 1).astype(F32)
    ident = jnp.broadcast_to(ident, (rows, 128)).astype(BF16)
    ident = mm(s.pack[...], ident).astype(BF16)
    packed = mm_nt(s.pack[...], states[last]).astype(BF16)
    for g in range(groups):
        s.out_late[g, :, 0:256] = packed[g * PAIR : (g + 1) * PAIR]
        s.out_late[g, :, 256:384] = ident[g * PAIR : (g + 1) * PAIR]

    pl.semaphore_wait(barrier, len(z_peers + y_peers + pop_peers))

    def exchange(source, target):
        sent = [
            wire.send(source.at[(p + k) % groups], target.at[p], device)
            for k, device in zip(range(1, groups), pop_peers)
        ]
        target[p] = source[p]
        return sent

    def exchanged(sent, target):
        for k, entry in zip(range(1, groups), sent):
            wire.arrived(entry, target.at[(p + groups - k) % groups])

    late = exchange(s.out_late, s.in_late)
    for t in range(last):
        packed = mm_nt(s.pack[...], states[t]).astype(BF16)
        for g in range(groups):
            s.out_early[g, t] = packed[g * PAIR : (g + 1) * PAIR]
    early = exchange(s.out_early, s.in_early)

    def factors(t):
        reset = jax.nn.sigmoid(gates[t, 0].astype(F32))
        cand_in = gates[t, 1].astype(F32)
        update = jax.nn.sigmoid(gates[t, 2].astype(F32) - 1.0)
        candidate = jnp.tanh(reset * cand_in)
        e = update * (1.0 - candidate * candidate)
        rest = 1.0 - update
        s.factor[t, 0] = e * cand_in * reset * (1.0 - reset)
        s.factor[t, 1] = e * reset
        s.factor[t, 2] = (candidate - states[t].astype(F32)) * update * rest
        s.factor[t, 3] = rest
        taken = actions[t].astype(F32)
        s.bound[t] = 1.0 - taken * taken

    factors(last)
    s.grad[...] = final_grad[...].astype(F32)

    def begin(t):
        for q in range(3):
            s.pre[q * 256 : (q + 1) * 256] = (s.grad[...] * s.factor[t, q]).astype(BF16)
        part = mm(jnp.concatenate([act_w[q] for q in range(3)], axis=1), s.pre[...])
        s.act_own[t, 0] = part.astype(BF16)
        return [
            wire.send(s.act_own.at[t, 0], s.act_in.at[t, 0, i], device)
            for i, device in enumerate(z_peers)
        ]

    def act_sum(t, stage, sent):
        for i, entry in enumerate(sent):
            wire.arrived(entry, s.act_in.at[t, stage, i])
        total = s.act_own[t, stage].astype(F32) + s.act_in[t, stage, 0].astype(F32)
        total = total + s.act_in[t, stage, 1].astype(F32)
        return total + s.act_in[t, stage, 2].astype(F32)

    def act_second(t, sent):
        s.act_own[t, 1] = act_sum(t, 0, sent).astype(BF16)
        return [
            wire.send(s.act_own.at[t, 1], s.act_in.at[t, 1, i], device)
            for i, device in enumerate(y_peers)
        ]

    def dispatch(t, sent):
        policy = (act_sum(t, 1, sent) * s.bound[t]).astype(BF16)
        packed = mm_nt(s.pack[...], policy).astype(BF16)
        for g in range(groups):
            s.policy_out[t, g] = packed[g * PAIR : (g + 1) * PAIR]
        return exchange(s.policy_out.at[t], s.policy_in.at[t])

    def collect(t, sent):
        exchanged(sent, s.policy_in.at[t])
        arrived = s.policy_in[t].reshape(pair_rows, 128)
        policy = mm(s.choose[...], arrived).astype(BF16)
        for m in range(members):
            s.policy[:, m * 128 : (m + 1) * 128] = policy * s.mask[m, :, 0:128]

    def store_blocks(b, total, lo):
        hi = lo + total.shape[1]
        s.held_a[b // RING, b % RING, :, lo:hi] = total[0:128]
        s.held_b[b % RING, b // RING, :, lo:hi] = total[128:256]

    def carried_part(lo):
        def two(i, carry):
            at = pl.ds(pl.multiple_of(i * 512, 512), 512)
            wide = jnp.concatenate([s.recur[q, at, :] for q in range(3)], axis=1)
            total = mm(wide, s.pre[...]).astype(BF16)
            store_blocks(2 * i, total[0:256], lo)
            store_blocks(2 * i + 1, total[256:512], lo)
            return carry

        lax.fori_loop(0, blocks // 2, two, 0)

    def weight_part(t, start):
        share = mm_nt(actions[t], s.pre[...])
        if start:
            s.weight[...] = share
        else:
            s.weight[...] += share

    def latents(t):
        if t == last:
            arrived = s.in_late[:, :, 0:256].reshape(pair_rows, 256)
        else:
            arrived = s.in_early[:, t].reshape(pair_rows, 256)
        chosen = mm(s.choose[...], arrived).T
        for m in range(members):
            s.latent[m * 256 : (m + 1) * 256] = jnp.where(s.names[0:1] == m + 1, chosen, 0.0).astype(BF16)

    def hidden_part(t, lo):
        latents(t)

        def two(i, carry):
            at = pl.ds(pl.multiple_of(i * 512, 512), 512)
            wide = jnp.concatenate([s.first[m, at, :] for m in range(members)], axis=1)
            total = mm(wide, s.latent[...]).astype(BF16)
            store_blocks(2 * i, total[0:256], lo)
            store_blocks(2 * i + 1, total[256:512], lo)
            return carry

        lax.fori_loop(0, blocks // 2, two, 0)

    def scatters(bufs, rest, lo, hi):
        one, two = bufs
        return [
            Scatter(wire, s.held_a, lo, hi, z_ring, y_ring, *one, rest[0]),
            Scatter(wire, s.held_b, lo, hi, y_ring, z_ring, *two, rest[1]),
        ]

    def slopes(t, pair, lo):
        hidden = jnp.concatenate([one.result(lo, lo + cap) for one in pair], axis=0)
        slope = silu_slope(hidden).T.astype(BF16)
        s.slope_a[t % 2, z, y] = slope[0:half]
        s.slope_b[t % 2, y, z] = slope[half:cap]
        return [
            Gather(wire, s.slope_a.at[t % 2], half, z_ring, y_ring),
            Gather(wire, s.slope_b.at[t % 2], half, y_ring, z_ring),
        ]

    def upward_part(i):
        at = pl.ds(pl.multiple_of(i * 1024, 1024), 1024)
        return mm(s.policy[...], s.second[:, at])

    def upward_ahead():
        def four(i, carry):
            s.upward[:, pl.ds(pl.multiple_of(i * 1024, 1024), 1024)] = upward_part(i)
            return carry

        lax.fori_loop(0, blocks // RING, four, 0)

    def backward(t, ahead):
        def four(i, carry):
            if ahead:
                upward = s.upward[:, pl.ds(pl.multiple_of(i * 1024, 1024), 1024)]
            else:
                upward = upward_part(i)
            for j in range(RING):
                at = pl.ds(pl.multiple_of(i * 1024 + j * 256, 256), 256)
                here = slice(j * 256, (j + 1) * 256)
                low = upward[0:half, here] * s.slope_a[t % 2, i, j].astype(F32)
                high = upward[half:cap, here] * s.slope_b[t % 2, j, i].astype(F32)
                s.scaled[0:half, at] = low.astype(BF16)
                s.scaled[half:cap, at] = high.astype(BF16)
            return carry

        lax.fori_loop(0, blocks // RING, four, 0)
        s.back[...] = jnp.zeros_like(s.back)

        def member(m, carry):
            s.back[...] += s.mask[m].astype(F32) * mm(s.scaled[...], s.first[m])
            return carry

        lax.fori_loop(0, members, member, 0)
        packed = mm(s.spread[...], s.back[...].astype(BF16)).astype(BF16)
        for g in range(groups):
            s.return_out[t, g] = packed[g * PAIR : (g + 1) * PAIR]
        return exchange(s.return_out.at[t], s.return_in.at[t])

    def finish(t, sent, pair, lo):
        exchanged(sent, s.return_in.at[t])
        own = mm(s.unpack[...], s.return_in[t].reshape(pair_rows, 256)).T
        direct = s.grad[...] * s.factor[t, 3]
        s.grad[0:128] = direct[0:128] + pair[0].result(lo, lo + 128) + own[0:128]
        s.grad[128:256] = direct[128:256] + pair[1].result(lo, lo + 128) + own[128:256]

    sends = []
    act = begin(last)

    exchanged(late, s.in_late)
    names_in = s.in_late[:, :, 256:384].reshape(pair_rows, 128)
    lane = lax.broadcasted_iota(jnp.int32, (8, 128), 1)
    picker = jnp.where(lane == 0, 1.0, 0.0).astype(BF16)
    names_row = mm_nt(picker, names_in)
    held_row = jnp.where(names_row > 0.5, 1.0, 0.0)
    a = lax.broadcasted_iota(jnp.int32, (pair_rows, pair_rows), 0)
    b = lax.broadcasted_iota(jnp.int32, (pair_rows, pair_rows), 1)
    place_row = mm(held_row.astype(BF16), jnp.where(a < b, 1.0, 0.0).astype(BF16))
    spot = lax.broadcasted_iota(jnp.int32, (cap, pair_rows), 0).astype(F32)
    chosen = jnp.where(spot == place_row[0:1], held_row[0:1], 0.0).astype(BF16)
    s.choose[...] = chosen
    held_col = jnp.where(names_in.astype(F32) > 0.5, 1.0, 0.0)
    place_col = mm(jnp.where(b < a, 1.0, 0.0).astype(BF16), held_col.astype(BF16))
    spot = lax.broadcasted_iota(jnp.int32, (pair_rows, cap), 1).astype(F32)
    chosen_t = jnp.where(spot == place_col[:, 0:1], held_col[:, 0:1], 0.0)
    s.spread[...] = chosen_t.astype(BF16)
    s.names[...] = mm(names_row.astype(BF16), s.spread[...])
    slot_name = mm(s.choose[...], names_in)
    for m in range(members):
        mask = jnp.where(jnp.abs(slot_name[:, 0:1] - (m + 1)) < 0.5, 1.0, 0.0)
        s.mask[m] = jnp.broadcast_to(mask, (cap, 256)).astype(BF16)

    def first_shares():
        for k in range(groups):
            s.share_out[k] = s.weight[k * 16 : (k + 1) * 16].astype(BF16)
        return exchange(s.share_out, s.share_in)

    def second_shares(shares):
        exchanged(shares, s.share_in)
        total = s.share_in[0].astype(F32)
        for k in range(1, groups):
            total = total + s.share_in[k].astype(F32)
        s.share_all[p] = total.astype(BF16)
        whole = [wire.send(s.share_all.at[p], s.share_all.at[p], device) for device in pop_peers]
        sends.extend(shares + whole)
        return whole

    def last_shares(whole):
        exchanged(whole, s.share_all)
        for k in range(groups):
            for q in range(3):
                weight_out[q, k * 16 : (k + 1) * 16] = s.share_all[k, :, q * 256 : (q + 1) * 256].astype(F32)

    def stage(pair, *numbers):
        for number in numbers:
            for one in pair:
                if number == 0:
                    one.stage0()
                else:
                    (one.stage1, one.stage2, one.stage3, one.stage4, one.landed)[number - 1]()

    loads[0].wait()
    if deep:
        early_lo, carried_lo, late_lo = 0, cap, cap + 128
        hidden_part(last, early_lo)
        opening = scatters(s.sums[steps], s.rests[1], early_lo, early_lo + cap)
        stage(opening, 0, 1)
        act2 = act_second(last, act)
        exchanged(early, s.in_early)
        hidden_part(last - 1, late_lo)
        second = scatters(s.sums[steps + 1], s.rests[0], late_lo, late_lo + cap)
        stage(opening, 2)
        stage(second, 0)
        loads[1].wait()
        carried_part(carried_lo)
        pair = scatters(s.sums[last], s.rests[2], carried_lo, late_lo)
        stage(opening, 3)
        stage(second, 1)
        out = dispatch(last, act2)
        weight_part(last, True)
        stage(opening, 4)
        stage(second, 2)
        stage(pair, 0, 1)
        stage(opening, 5)
        gather = slopes(last, opening, 0)
        stage(gather, 1)
        stage(second, 3)
        stage(pair, 2)
        hidden_part(last - 2, early_lo)
        later = scatters(s.sums[steps + 2], s.rests[1], early_lo, early_lo + cap)
        stage(gather, 2)
        stage(second, 4)
        stage(pair, 3)
        loads[2].wait()
        collect(last, out)
        upward_ahead()
        stage(gather, 3)
        stage(second, 5)
        following = slopes(last - 1, second, 0)
        stage(pair, 4)
        for t in range(last):
            factors(t)
        stage(gather, 4)
        stage(following, 1)
        stage(later, 0, 1)
        stage(gather, 5)
        stage(following, 2)
        sends += act + act2 + late + early + out
        back = backward(last, True)
        stage(later, 2)
        stage(following, 3)
        hidden_part(0, late_lo)
        for t in range(last, -1, -1):
            if t < last:
                gather = following
                act = begin(t)
                carried_part(carried_lo)
                pair = scatters(s.sums[t], s.rests[2], carried_lo, late_lo)
                if t > 0:
                    stage(later, 3)
                act2 = act_second(t, act)
                stage(pair, 0, 1)
                if t > 0:
                    stage(later, 4)
                stage(gather, 4)
                weight_part(t, False)
                if t == 0:
                    shares = first_shares()
                out = dispatch(t, act2)
                sends += act + act2 + out
                stage(pair, 2)
                if t > 0:
                    stage(later, 5)
                    following = slopes(t - 1, later, 0)
                    stage(following, 1)
                if t == last - 1:
                    later = scatters(s.sums[steps + 3], s.rests[0], late_lo, late_lo + cap)
                    stage(later, 0, 1)
                collect(t, out)
                stage(pair, 3)
                if t == 0:
                    whole = second_shares(shares)
                if t > 0:
                    stage(following, 2)
                stage(gather, 5)
                back = backward(t, False)
                stage(pair, 4)
                if t == last - 1:
                    stage(later, 2)
                if t > 0:
                    stage(following, 3)
            sends += back
            stage(pair, 5)
            if t == 0:
                last_shares(whole)
            finish(t, back, pair, 0)
    else:
        hidden_part(last, 128)
        opening = scatters(s.sums[steps], s.rests[0], 128, 128 + cap)
        stage(opening, 0, 1)
        act2 = act_second(last, act)
        loads[1].wait()
        carried_part(0)
        stage(opening, 2)
        out = dispatch(last, act2)
        weight_part(last, True)
        stage(opening, 3)
        for t in range(last):
            factors(t)
        exchanged(early, s.in_early)
        stage(opening, 4)
        loads[2].wait()
        collect(last, out)
        stage(opening, 5)
        gather = slopes(last, opening, 0)
        stage(gather, 1)
        hidden_part(last - 1, 128)
        pair = scatters(s.sums[last], s.rests[0], 0, 128 + cap)
        stage(pair, 0)
        for number in range(1, 5):
            stage(pair, number)
            stage(gather, number + 1)
        sends += act + act2 + late + early + out
        for t in range(last, -1, -1):
            if t < last:
                act = begin(t)
                pair = scatters(s.sums[t], s.rests[0], 0, 128 + cap if t > 0 else 128)
                carried_part(0)
                stage(pair, 0, 1)
                stage(gather, 3)
                act2 = act_second(t, act)
                weight_part(t, False)
                stage(pair, 2)
                stage(gather, 4)
                if t == 0:
                    shares = first_shares()
                out = dispatch(t, act2)
                stage(pair, 3)
                sends += act + act2 + out
                collect(t, out)
                stage(pair, 4)
                if t == 0:
                    whole = second_shares(shares)
                stage(gather, 5)
            back = backward(t, False)
            sends += back
            stage(pair, 5)
            if t > 0:
                gather = slopes(t - 1, pair, 128)
                stage(gather, 1)
                if t > 1:
                    hidden_part(t - 2, 128)
                stage(gather, 2)
            else:
                last_shares(whole)
            finish(t, back, pair, 0)
    start_out[...] = s.grad[...].astype(BF16)
    wait_sends(sends)


def sum_bufs(width):
    def four():
        return (
            pltpu.VMEM((2, 2, 128, width), BF16),
            pltpu.VMEM((2, RING, 128, width), BF16),
            pltpu.VMEM((2, 64, width), BF16),
            pltpu.VMEM((2, 128, width), BF16),
        )

    return four(), four()


def scratch_shapes(steps, cap, deep, groups, members, blocks):
    half = cap // 2
    held = 128 + 2 * cap if deep else 128 + cap
    v = pltpu.VMEM
    shapes = dict(
        first=v((members, blocks * 256, 256), BF16),
        recur=v((3, blocks * 256, 256), BF16),
        second=v((members * 128, blocks * 256), BF16),
        pack=v((groups * PAIR, 128), BF16),
        unpack=v((128, groups * PAIR), BF16),
        choose=v((cap, groups * PAIR), BF16),
        spread=v((groups * PAIR, cap), BF16),
        mask=v((members, cap, 256), BF16),
        out_late=v((groups, PAIR, 384), BF16),
        in_late=v((groups, PAIR, 384), BF16),
        out_early=v((groups, steps - 1, PAIR, 256), BF16),
        in_early=v((groups, steps - 1, PAIR, 256), BF16),
        factor=v((steps, 4, 256, 128), F32),
        bound=v((steps, 128, 128), F32),
        grad=v((256, 128), F32),
        pre=v((768, 128), BF16),
        act_own=v((steps, 2, 128, 128), BF16),
        act_in=v((steps, 2, 3, 128, 128), BF16),
        policy_out=v((steps, groups, PAIR, 128), BF16),
        policy_in=v((steps, groups, PAIR, 128), BF16),
        policy=v((cap, members * 128), BF16),
        latent=v((members * 256, cap), BF16),
        names=v((8, cap), F32),
        scaled=v((cap, blocks * 256), BF16),
        weight=v((128, 768), F32),
        share_out=v((groups, 16, 768), BF16),
        share_in=v((groups, 16, 768), BF16),
        share_all=v((groups, 16, 768), BF16),
        back=v((cap, 256), F32),
        return_out=v((steps, groups, PAIR, 256), BF16),
        return_in=v((steps, groups, PAIR, 256), BF16),
        held_a=v((RING, RING, 128, held), BF16),
        held_b=v((RING, RING, 128, held), BF16),
        slope_a=v((2, RING, RING, half, 256), BF16),
        slope_b=v((2, RING, RING, half, 256), BF16),
    )
    if deep:
        widths = [128] * steps + [cap] * steps
        rests = (cap, cap, 128)
        shapes.update(upward=v((cap, blocks * 256), F32))
    else:
        widths = [128] + [128 + cap] * (steps - 1) + [cap]
        rests = (128 + cap,)
    shapes.update(
        sums=[sum_bufs(width) for width in widths],
        rests=[[v((RING, 128, width), BF16) for side in range(2)] for width in rests],
    )
    copies = 4 * (groups - 1) + 2 * steps * 24 + steps * (16 + 6 + 2 * (groups - 1))
    shapes.update(send_sems=pltpu.SemaphoreType.DMA((copies,)))
    shapes.update(recv_sems=pltpu.SemaphoreType.DMA((copies,)))
    shapes.update(load_sems=pltpu.SemaphoreType.DMA((3,)))
    return shapes


def call(cap, deep, groups, blocks, name, collective_id):
    def run(states, gates, actions, final_grad, act_w, opp_row, opp_col, recur, first, second):
        steps, members = states.shape[0], first.shape[0]
        vmem = pl.BlockSpec(memory_space=pltpu.VMEM)
        hbm = pl.BlockSpec(memory_space=pl.ANY)
        return pl.pallas_call(
            functools.partial(kernel, steps, cap, deep, groups, members, blocks),
            out_shape=(
                jax.ShapeDtypeStruct((256, 128), BF16),
                jax.ShapeDtypeStruct((3, 128, 256), F32),
            ),
            in_specs=[vmem] * 7 + [hbm] * 3,
            out_specs=(vmem, vmem),
            scratch_shapes=jax.tree.leaves(scratch_shapes(steps, cap, deep, groups, members, blocks)),
            compiler_params=pltpu.CompilerParams(
                collective_id=collective_id, has_side_effects=True, vmem_limit_bytes=62 << 20
            ),
            name=name,
        )(states, gates, actions, final_grad, act_w, opp_row, opp_col, recur, first, second)

    return run


def body(
    states,
    gate_inputs,
    actions,
    final_grad,
    recur_weight,
    act_weight,
    opp_first,
    opp_second,
    opponent,
):
    groups = lax.axis_size("pop")
    blocks = lax.axis_size("unit")
    recur = jnp.transpose(recur_weight, (1, 0, 2))
    act_w = jnp.transpose(act_weight, (1, 0, 2))
    operands = (
        states,
        gate_inputs,
        actions,
        final_grad,
        act_w,
        opponent.reshape(1, -1),
        opponent,
        recur,
        opp_first,
        opp_second.reshape(-1, opp_second.shape[2]),
    )
    everyone = lax.all_gather(opponent[:, 0], "pop").reshape(1, -1)
    named = everyone // opp_first.shape[0] == jnp.arange(groups, dtype=jnp.int32)[:, None]
    most = jnp.max(jnp.sum(named.astype(jnp.int32), axis=1))
    start, weight = lax.cond(
        most <= FEW,
        call(FEW, True, groups, blocks, "few_slots", 0),
        call(groups * PAIR, False, groups, blocks, "all_slots", 1),
        *operands,
    )
    return start, jnp.transpose(weight, (1, 0, 2))


def solution(mesh):
    placed = (
        P(None, "unit", "pop"),
        P(None, None, "unit", "pop"),
        P(None, None, "pop"),
        P("unit", "pop"),
        P(None, None, "unit"),
        P(None, None, "unit"),
        P("pop", None, "unit"),
        P("pop", None, None),
        P("pop", None),
    )
    return jax.shard_map(
        body,
        mesh=mesh,
        in_specs=placed,
        out_specs=(P("unit", "pop"), P(None, None, "unit")),
        check_vma=False,
    )
```

```python
import functools
import types

import jax
import jax.numpy as jnp
from jax import lax
from jax.experimental import pallas as pl
from jax.experimental.pallas import tpu as pltpu
from jax.sharding import PartitionSpec as P

MESH = pl.DeviceIdType.MESH
F32 = jnp.float32
BF16 = jnp.bfloat16
PAIR = 48
FEW = 256
RING = 4


def mm(a, b):
    return jnp.dot(a, b, preferred_element_type=F32)


def mm_nt(a, b):
    return lax.dot_general(a, b, (((1,), (1,)), ((), ())), preferred_element_type=F32)


def silu_slope(values):
    logistic = jax.nn.sigmoid(values)
    return logistic * (1.0 + values * (1.0 - logistic))


class Wire:
    def __init__(self, send_sems, recv_sems):
        self.send_sems = send_sems
        self.recv_sems = recv_sems
        self.count = 0

    def send(self, source, target, device):
        number = self.count
        self.count += 1
        copy = pltpu.make_async_remote_copy(
            src_ref=source,
            dst_ref=target,
            send_sem=self.send_sems.at[number],
            recv_sem=self.recv_sems.at[number],
            device_id=device,
            device_id_type=MESH,
        )
        copy.start()
        return copy, number, device

    def arrived(self, sent, landing):
        pltpu.make_async_remote_copy(
            src_ref=landing,
            dst_ref=landing,
            send_sem=self.send_sems.at[sent[1]],
            recv_sem=self.recv_sems.at[sent[1]],
            device_id=sent[2],
            device_id_type=MESH,
        ).wait_recv()


def wait_sends(sent):
    for entry in sent:
        entry[0].wait_send()


class Scatter:
    def __init__(self, wire, held, lo, hi, first, second, one, two, three, four, rest):
        self.wire, self.held, self.lo, self.hi = wire, held, lo, hi
        self.first, self.second = first, second
        self.one, self.two, self.three, self.four, self.rest = one, two, three, four, rest
        self.width = hi - lo

    def part(self, index, a, b):
        return self.held.at[index, a:b, :, self.lo : self.hi]

    def line(self, index, a, b):
        return self.rest.at[index, a:b, 0 : self.width]

    def stage0(self):
        w, (me, plus, minus) = self.wire, self.first
        far = (me + 2) % RING
        self.s0 = [
            w.send(self.part(far, 0, 2), self.one.at[0], plus),
            w.send(self.part(far, 2, 4), self.one.at[1], minus),
        ]

    def stage1(self):
        w, (me, plus, minus) = self.wire, self.first
        up, down = (me + 1) % RING, (me + 3) % RING
        self.s1 = [
            w.send(self.part(up, 2, 4), self.two.at[0, 2:4], plus),
            w.send(self.part(down, 0, 2), self.two.at[1, 0:2], minus),
        ]

    def stage2(self):
        w, (me, plus, minus) = self.wire, self.first
        up, down = (me + 1) % RING, (me + 3) % RING
        lo, hi = self.lo, self.hi
        self.s2 = []
        for side, block, base, device in ((0, up, 0, plus), (1, down, 2, minus)):
            w.arrived(self.s0[side], self.one.at[side])

            def add(i, carry, side=side, block=block, base=base):
                total = self.held[block, base + i, :, lo:hi].astype(F32)
                total = total + self.one[side, i].astype(F32)
                self.held[block, base + i, :, lo:hi] = total.astype(BF16)
                return carry

            lax.fori_loop(0, 2, add, 0)
            self.s2.append(
                w.send(
                    self.part(block, base, base + 2), self.two.at[side, base : base + 2], device
                )
            )

    def stage3(self):
        w, me = self.wire, self.first[0]
        at, plus, minus = self.second
        lo, hi = self.lo, self.hi
        w.arrived(self.s1[0], self.two.at[0, 2:4])
        w.arrived(self.s1[1], self.two.at[1, 0:2])
        w.arrived(self.s2[0], self.two.at[0, 0:2])
        w.arrived(self.s2[1], self.two.at[1, 2:4])

        def add(i, carry):
            total = self.held[me, i, :, lo:hi].astype(F32) + self.two[0, i].astype(F32)
            total = total + self.two[1, i].astype(F32)
            self.rest[i, :, 0 : self.width] = total.astype(BF16)
            return carry

        lax.fori_loop(0, RING, add, 0)
        up, down, far = (at + 1) % RING, (at + 3) % RING, (at + 2) % RING
        self.s3 = [
            w.send(self.line(far, 0, 64), self.three.at[0], plus),
            w.send(self.line(far, 64, 128), self.three.at[1], minus),
            w.send(self.line(up, 64, 128), self.four.at[0, 64:128], plus),
            w.send(self.line(down, 0, 64), self.four.at[1, 0:64], minus),
        ]

    def stage4(self):
        w = self.wire
        at, plus, minus = self.second
        up, down = (at + 1) % RING, (at + 3) % RING
        self.s4 = []
        for side, block, base, device in ((0, up, 0, plus), (1, down, 64, minus)):
            w.arrived(self.s3[side], self.three.at[side])
            total = self.rest[block, base : base + 64, 0 : self.width].astype(F32)
            total = total + self.three[side].astype(F32)
            self.rest[block, base : base + 64, 0 : self.width] = total.astype(BF16)
            self.s4.append(
                w.send(
                    self.line(block, base, base + 64), self.four.at[side, base : base + 64], device
                )
            )

    def landed(self):
        w = self.wire
        w.arrived(self.s3[2], self.four.at[0, 64:128])
        w.arrived(self.s3[3], self.four.at[1, 0:64])
        w.arrived(self.s4[0], self.four.at[0, 0:64])
        w.arrived(self.s4[1], self.four.at[1, 64:128])
        wait_sends(self.s0 + self.s1 + self.s2 + self.s3 + self.s4)

    def result(self, a, b):
        total = self.rest[self.second[0], :, a:b].astype(F32) + self.four[0, :, a:b].astype(F32)
        return total + self.four[1, :, a:b].astype(F32)


class Gather:
    def __init__(self, wire, held, rows, first, second):
        self.wire, self.held, self.rows = wire, held, rows
        self.first, self.second = first, second

    def stage1(self):
        f, (at, plus, minus) = self.first[0], self.second
        own = self.held.at[f, at]
        self.a1 = [self.wire.send(own, own, plus), self.wire.send(own, own, minus)]

    def stage2(self):
        f, (at, plus, minus) = self.first[0], self.second
        half = self.rows // 2
        below, above = (at + 3) % RING, (at + 1) % RING
        self.wire.arrived(self.a1[0], self.held.at[f, below])
        low = self.held.at[f, below, 0:half]
        first = self.wire.send(low, low, plus)
        self.wire.arrived(self.a1[1], self.held.at[f, above])
        high = self.held.at[f, above, half : 2 * half]
        self.a2 = [first, self.wire.send(high, high, minus)]

    def stage3(self):
        f, plus, minus = self.first
        at = self.second[0]
        half = self.rows // 2
        far = (at + 2) % RING
        self.wire.arrived(self.a2[0], self.held.at[f, far, 0:half])
        self.wire.arrived(self.a2[1], self.held.at[f, far, half : 2 * half])
        line = self.held.at[f]
        self.a3 = [self.wire.send(line, line, plus), self.wire.send(line, line, minus)]

    def stage4(self):
        f, plus, minus = self.first
        below, above = (f + 3) % RING, (f + 1) % RING
        self.wire.arrived(self.a3[0], self.held.at[below])
        low = self.held.at[below, 0:2]
        first = self.wire.send(low, low, plus)
        self.wire.arrived(self.a3[1], self.held.at[above])
        high = self.held.at[above, 2:4]
        self.a4 = [first, self.wire.send(high, high, minus)]

    def landed(self):
        far = (self.first[0] + 2) % RING
        self.wire.arrived(self.a4[0], self.held.at[far, 0:2])
        self.wire.arrived(self.a4[1], self.held.at[far, 2:4])
        wait_sends(self.a1 + self.a2 + self.a3 + self.a4)


def pair_slots(chosen, groups, members):
    rows = chosen.shape[1]
    group_of = (chosen // members).astype(F32)
    index = lax.broadcasted_iota(jnp.int32, (groups, rows), 0).astype(F32)
    onehot = jnp.where(group_of == index, 1.0, 0.0)
    a = lax.broadcasted_iota(jnp.int32, (rows, rows), 0)
    b = lax.broadcasted_iota(jnp.int32, (rows, rows), 1)
    rank = mm(onehot.astype(BF16), jnp.where(a < b, 1.0, 0.0).astype(BF16))
    key = jnp.sum(onehot * (rank + index * PAIR), axis=0, keepdims=True)
    slot = lax.broadcasted_iota(jnp.int32, (groups * PAIR, rows), 0).astype(F32)
    return jnp.where(slot == key, 1.0, 0.0)


def to_groups(wire, groups, peers, p, source, target):
    sent = [
        wire.send(source.at[(p + k) % groups], target.at[p], device)
        for k, device in zip(range(1, groups), peers)
    ]
    target[p] = source[p]
    return sent


def from_groups(wire, groups, p, sent, target):
    for k, entry in zip(range(1, groups), sent):
        wire.arrived(entry, target.at[(p + groups - k) % groups])


def spread_kernel(
    steps,
    groups,
    members,
    states,
    opp_row,
    late,
    everyone,
    pack,
    out_late,
    named,
    send_sems,
    recv_sems,
):
    p = lax.axis_index("pop")
    u = lax.axis_index("unit")
    peers = [((p + k) % groups, u) for k in range(1, groups)]
    barrier = pltpu.get_barrier_semaphore()
    for device in peers:
        pl.semaphore_signal(barrier, inc=1, device_id=device, device_id_type=MESH)
    wire = Wire(send_sems, recv_sems)
    named[...] = jnp.broadcast_to(opp_row[...], named.shape)
    pack[...] = pair_slots(opp_row[...], groups, members).astype(BF16)
    ident = jnp.broadcast_to((opp_row[...] % members + 1).astype(F32), (128, 128)).astype(BF16)
    ident = mm_nt(pack[...], ident).astype(BF16)
    last = steps - 1
    packed = mm_nt(pack[...], states[last]).astype(BF16)
    for g in range(groups):
        out_late[g, :, 0:256] = packed[g * PAIR : (g + 1) * PAIR]
        out_late[g, :, 256:384] = ident[g * PAIR : (g + 1) * PAIR]
    pl.semaphore_wait(barrier, len(peers))
    names = [wire.send(named, everyone.at[p], device) for device in peers]
    everyone[p] = named[...]
    lates = to_groups(wire, groups, peers, p, out_late, late)
    from_groups(wire, groups, p, names, everyone)
    from_groups(wire, groups, p, lates, late)
    wait_sends(names + lates)


def spread(states, opp_row, groups, members):
    steps = states.shape[0]
    vmem = pl.BlockSpec(memory_space=pltpu.VMEM)
    shape = (groups, PAIR, 384)
    copies = 2 * (groups - 1)
    return pl.pallas_call(
        functools.partial(spread_kernel, steps, groups, members),
        out_shape=[
            jax.ShapeDtypeStruct(shape, BF16),
            jax.ShapeDtypeStruct((groups, 8, 128), jnp.int32),
        ],
        in_specs=[vmem] * 2,
        out_specs=[vmem] * 2,
        scratch_shapes=[
            pltpu.VMEM((groups * PAIR, 128), BF16),
            pltpu.VMEM(shape, BF16),
            pltpu.VMEM((8, 128), jnp.int32),
            pltpu.SemaphoreType.DMA((copies,)),
            pltpu.SemaphoreType.DMA((copies,)),
        ],
        compiler_params=pltpu.CompilerParams(
            collective_id=2, has_side_effects=True, vmem_limit_bytes=16 << 20
        ),
        name="spread",
    )(states, opp_row)


def kernel(
    steps,
    cap,
    deep,
    groups,
    members,
    blocks,
    states,
    gates,
    actions,
    final_grad,
    act_w,
    opp_row,
    in_late,
    recur_hbm,
    first_hbm,
    second_hbm,
    start_out,
    weight_out,
    *scratch,
):
    shapes = scratch_shapes(steps, cap, deep, groups, members, blocks)
    s = types.SimpleNamespace(**jax.tree.unflatten(jax.tree.structure(shapes), scratch))
    rows = 128
    half = cap // 2
    last = steps - 1
    pair_rows = groups * PAIR
    p = lax.axis_index("pop")
    u = lax.axis_index("unit")
    z, y = u // RING, u % RING

    def at_unit(zz, yy):
        return (p, (zz % RING) * RING + yy % RING)

    z_ring = (z, at_unit(z + 1, y), at_unit(z + 3, y))
    y_ring = (y, at_unit(z, y + 1), at_unit(z, y + 3))
    z_peers = [at_unit(z + k, y) for k in (1, 2, 3)]
    y_peers = [at_unit(z, y + k) for k in (1, 2, 3)]
    pop_peers = [((p + k) % groups, u) for k in range(1, groups)]
    barrier = pltpu.get_barrier_semaphore()
    for device in z_peers + y_peers + pop_peers:
        pl.semaphore_signal(barrier, inc=1, device_id=device, device_id_type=MESH)

    loads = [
        pltpu.make_async_copy(first_hbm, s.first, s.load_sems.at[0]),
        pltpu.make_async_copy(recur_hbm, s.recur, s.load_sems.at[1]),
        pltpu.make_async_copy(second_hbm, s.second, s.load_sems.at[2]),
    ]
    for load in loads:
        load.start()
    wire = Wire(s.send_sems, s.recv_sems)

    pack = pair_slots(opp_row[...], groups, members)
    s.pack[...] = pack.astype(BF16)
    s.unpack[...] = pack.T.astype(BF16)

    pl.semaphore_wait(barrier, len(z_peers + y_peers + pop_peers))

    def exchange(source, target):
        return to_groups(wire, groups, pop_peers, p, source, target)

    def exchanged(sent, target):
        from_groups(wire, groups, p, sent, target)

    for t in range(last):
        packed = mm_nt(s.pack[...], states[t]).astype(BF16)
        for g in range(groups):
            s.out_early[g, t] = packed[g * PAIR : (g + 1) * PAIR]
    early = exchange(s.out_early, s.in_early)

    def factors(t):
        reset = jax.nn.sigmoid(gates[t, 0].astype(F32))
        cand_in = gates[t, 1].astype(F32)
        update = jax.nn.sigmoid(gates[t, 2].astype(F32) - 1.0)
        candidate = jnp.tanh(reset * cand_in)
        e = update * (1.0 - candidate * candidate)
        rest = 1.0 - update
        s.factor[t, 0] = e * cand_in * reset * (1.0 - reset)
        s.factor[t, 1] = e * reset
        s.factor[t, 2] = (candidate - states[t].astype(F32)) * update * rest
        s.factor[t, 3] = rest
        taken = actions[t].astype(F32)
        s.bound[t] = 1.0 - taken * taken

    factors(last)
    s.grad[...] = final_grad[...].astype(F32)

    def begin(t):
        for q in range(3):
            s.pre[q * 256 : (q + 1) * 256] = (s.grad[...] * s.factor[t, q]).astype(BF16)
        part = mm(jnp.concatenate([act_w[q] for q in range(3)], axis=1), s.pre[...])
        s.act_own[t, 0] = part.astype(BF16)
        return [
            wire.send(s.act_own.at[t, 0], s.act_in.at[t, 0, i], device)
            for i, device in enumerate(z_peers)
        ]

    def act_sum(t, stage, sent):
        for i, entry in enumerate(sent):
            wire.arrived(entry, s.act_in.at[t, stage, i])
        total = s.act_own[t, stage].astype(F32) + s.act_in[t, stage, 0].astype(F32)
        total = total + s.act_in[t, stage, 1].astype(F32)
        return total + s.act_in[t, stage, 2].astype(F32)

    def act_second(t, sent):
        s.act_own[t, 1] = act_sum(t, 0, sent).astype(BF16)
        return [
            wire.send(s.act_own.at[t, 1], s.act_in.at[t, 1, i], device)
            for i, device in enumerate(y_peers)
        ]

    def dispatch(t, sent):
        policy = (act_sum(t, 1, sent) * s.bound[t]).astype(BF16)
        packed = mm_nt(s.pack[...], policy).astype(BF16)
        for g in range(groups):
            s.policy_out[t, g] = packed[g * PAIR : (g + 1) * PAIR]
        return exchange(s.policy_out.at[t], s.policy_in.at[t])

    def collect(t, sent):
        exchanged(sent, s.policy_in.at[t])
        arrived = s.policy_in[t].reshape(pair_rows, 128)
        policy = mm(s.choose[...], arrived).astype(BF16)
        for m in range(members):
            s.policy[:, m * 128 : (m + 1) * 128] = policy * s.mask[m, :, 0:128]

    def store_blocks(b, total, lo):
        hi = lo + total.shape[1]
        s.held_a[b // RING, b % RING, :, lo:hi] = total[0:128]
        s.held_b[b % RING, b // RING, :, lo:hi] = total[128:256]

    def carried_part(lo):
        def two(i, carry):
            at = pl.ds(pl.multiple_of(i * 512, 512), 512)
            wide = jnp.concatenate([s.recur[q, at, :] for q in range(3)], axis=1)
            total = mm(wide, s.pre[...]).astype(BF16)
            store_blocks(2 * i, total[0:256], lo)
            store_blocks(2 * i + 1, total[256:512], lo)
            return carry

        lax.fori_loop(0, blocks // 2, two, 0)

    def weight_part(t, start):
        share = mm_nt(actions[t], s.pre[...])
        if start:
            s.weight[...] = share
        else:
            s.weight[...] += share

    def latents(t):
        if t == last:
            arrived = in_late[:, :, 0:256].reshape(pair_rows, 256)
        else:
            arrived = s.in_early[:, t].reshape(pair_rows, 256)
        chosen = mm(s.choose[...], arrived).T
        for m in range(members):
            s.latent[m * 256 : (m + 1) * 256] = jnp.where(s.names[0:1] == m + 1, chosen, 0.0).astype(BF16)

    def hidden_part(t, lo):
        latents(t)

        def two(i, carry):
            at = pl.ds(pl.multiple_of(i * 512, 512), 512)
            wide = jnp.concatenate([s.first[m, at, :] for m in range(members)], axis=1)
            total = mm(wide, s.latent[...]).astype(BF16)
            store_blocks(2 * i, total[0:256], lo)
            store_blocks(2 * i + 1, total[256:512], lo)
            return carry

        lax.fori_loop(0, blocks // 2, two, 0)

    def scatters(bufs, rest, lo, hi):
        one, two = bufs
        return [
            Scatter(wire, s.held_a, lo, hi, z_ring, y_ring, *one, rest[0]),
            Scatter(wire, s.held_b, lo, hi, y_ring, z_ring, *two, rest[1]),
        ]

    def slopes(t, pair, lo):
        hidden = jnp.concatenate([one.result(lo, lo + cap) for one in pair], axis=0)
        slope = silu_slope(hidden).T.astype(BF16)
        s.slope_a[t % 2, z, y] = slope[0:half]
        s.slope_b[t % 2, y, z] = slope[half:cap]
        return [
            Gather(wire, s.slope_a.at[t % 2], half, z_ring, y_ring),
            Gather(wire, s.slope_b.at[t % 2], half, y_ring, z_ring),
        ]

    def upward_part(i):
        at = pl.ds(pl.multiple_of(i * 1024, 1024), 1024)
        return mm(s.policy[...], s.second[:, at])

    def upward_ahead():
        def four(i, carry):
            s.upward[:, pl.ds(pl.multiple_of(i * 1024, 1024), 1024)] = upward_part(i)
            return carry

        lax.fori_loop(0, blocks // RING, four, 0)

    def backward(t, ahead):
        def four(i, carry):
            if ahead:
                upward = s.upward[:, pl.ds(pl.multiple_of(i * 1024, 1024), 1024)]
            else:
                upward = upward_part(i)
            for j in range(RING):
                at = pl.ds(pl.multiple_of(i * 1024 + j * 256, 256), 256)
                here = slice(j * 256, (j + 1) * 256)
                low = upward[0:half, here] * s.slope_a[t % 2, i, j].astype(F32)
                high = upward[half:cap, here] * s.slope_b[t % 2, j, i].astype(F32)
                s.scaled[0:half, at] = low.astype(BF16)
                s.scaled[half:cap, at] = high.astype(BF16)
            return carry

        lax.fori_loop(0, blocks // RING, four, 0)
        s.back[...] = jnp.zeros_like(s.back)

        def member(m, carry):
            s.back[...] += s.mask[m].astype(F32) * mm(s.scaled[...], s.first[m])
            return carry

        lax.fori_loop(0, members, member, 0)
        packed = mm(s.spread[...], s.back[...].astype(BF16)).astype(BF16)
        for g in range(groups):
            s.return_out[t, g] = packed[g * PAIR : (g + 1) * PAIR]
        return exchange(s.return_out.at[t], s.return_in.at[t])

    def finish(t, sent, pair, lo):
        exchanged(sent, s.return_in.at[t])
        own = mm(s.unpack[...], s.return_in[t].reshape(pair_rows, 256)).T
        direct = s.grad[...] * s.factor[t, 3]
        s.grad[0:128] = direct[0:128] + pair[0].result(lo, lo + 128) + own[0:128]
        s.grad[128:256] = direct[128:256] + pair[1].result(lo, lo + 128) + own[128:256]

    sends = []
    act = begin(last)

    names_in = in_late[:, :, 256:384].reshape(pair_rows, 128)
    lane = lax.broadcasted_iota(jnp.int32, (8, 128), 1)
    picker = jnp.where(lane == 0, 1.0, 0.0).astype(BF16)
    names_row = mm_nt(picker, names_in)
    held_row = jnp.where(names_row > 0.5, 1.0, 0.0)
    a = lax.broadcasted_iota(jnp.int32, (pair_rows, pair_rows), 0)
    b = lax.broadcasted_iota(jnp.int32, (pair_rows, pair_rows), 1)
    place_row = mm(held_row.astype(BF16), jnp.where(a < b, 1.0, 0.0).astype(BF16))
    spot = lax.broadcasted_iota(jnp.int32, (cap, pair_rows), 0).astype(F32)
    chosen = jnp.where(spot == place_row[0:1], held_row[0:1], 0.0).astype(BF16)
    s.choose[...] = chosen
    held_col = jnp.where(names_in.astype(F32) > 0.5, 1.0, 0.0)
    place_col = mm(jnp.where(b < a, 1.0, 0.0).astype(BF16), held_col.astype(BF16))
    spot = lax.broadcasted_iota(jnp.int32, (pair_rows, cap), 1).astype(F32)
    chosen_t = jnp.where(spot == place_col[:, 0:1], held_col[:, 0:1], 0.0)
    s.spread[...] = chosen_t.astype(BF16)
    s.names[...] = mm(names_row.astype(BF16), s.spread[...])
    slot_name = mm(s.choose[...], names_in)
    for m in range(members):
        mask = jnp.where(jnp.abs(slot_name[:, 0:1] - (m + 1)) < 0.5, 1.0, 0.0)
        s.mask[m] = jnp.broadcast_to(mask, (cap, 256)).astype(BF16)

    def first_shares():
        for k in range(groups):
            s.share_out[k] = s.weight[k * 16 : (k + 1) * 16].astype(BF16)
        return exchange(s.share_out, s.share_in)

    def second_shares(shares):
        exchanged(shares, s.share_in)
        total = s.share_in[0].astype(F32)
        for k in range(1, groups):
            total = total + s.share_in[k].astype(F32)
        s.share_all[p] = total.astype(BF16)
        whole = [wire.send(s.share_all.at[p], s.share_all.at[p], device) for device in pop_peers]
        sends.extend(shares + whole)
        return whole

    def last_shares(whole):
        exchanged(whole, s.share_all)
        for k in range(groups):
            for q in range(3):
                weight_out[q, k * 16 : (k + 1) * 16] = s.share_all[k, :, q * 256 : (q + 1) * 256].astype(F32)

    def stage(pair, *numbers):
        for number in numbers:
            for one in pair:
                if number == 0:
                    one.stage0()
                else:
                    (one.stage1, one.stage2, one.stage3, one.stage4, one.landed)[number - 1]()

    loads[0].wait()
    if deep:
        early_lo, carried_lo, late_lo = 0, cap, cap + 128
        hidden_part(last, early_lo)
        opening = scatters(s.sums[steps], s.rests[1], early_lo, early_lo + cap)
        stage(opening, 0, 1)
        act2 = act_second(last, act)
        exchanged(early, s.in_early)
        hidden_part(last - 1, late_lo)
        second = scatters(s.sums[steps + 1], s.rests[0], late_lo, late_lo + cap)
        stage(opening, 2)
        stage(second, 0)
        loads[1].wait()
        carried_part(carried_lo)
        pair = scatters(s.sums[last], s.rests[2], carried_lo, late_lo)
        stage(opening, 3)
        stage(second, 1)
        out = dispatch(last, act2)
        weight_part(last, True)
        stage(opening, 4)
        stage(second, 2)
        stage(pair, 0, 1)
        stage(opening, 5)
        gather = slopes(last, opening, 0)
        stage(gather, 1)
        stage(second, 3)
        stage(pair, 2)
        hidden_part(last - 2, early_lo)
        later = scatters(s.sums[steps + 2], s.rests[1], early_lo, early_lo + cap)
        stage(gather, 2)
        stage(second, 4)
        stage(pair, 3)
        loads[2].wait()
        collect(last, out)
        upward_ahead()
        stage(gather, 3)
        stage(second, 5)
        following = slopes(last - 1, second, 0)
        stage(pair, 4)
        for t in range(last):
            factors(t)
        stage(gather, 4)
        stage(following, 1)
        stage(later, 0, 1)
        stage(gather, 5)
        stage(following, 2)
        sends += act + act2 + out + early
        back = backward(last, True)
        stage(later, 2)
        stage(following, 3)
        hidden_part(0, late_lo)
        for t in range(last, -1, -1):
            if t < last:
                gather = following
                act = begin(t)
                carried_part(carried_lo)
                pair = scatters(s.sums[t], s.rests[2], carried_lo, late_lo)
                if t > 0:
                    stage(later, 3)
                act2 = act_second(t, act)
                stage(pair, 0, 1)
                if t > 0:
                    stage(later, 4)
                stage(gather, 4)
                weight_part(t, False)
                if t == 0:
                    shares = first_shares()
                out = dispatch(t, act2)
                sends += act + act2 + out
                stage(pair, 2)
                if t > 0:
                    stage(later, 5)
                    following = slopes(t - 1, later, 0)
                    stage(following, 1)
                if t == last - 1:
                    later = scatters(s.sums[steps + 3], s.rests[0], late_lo, late_lo + cap)
                    stage(later, 0, 1)
                collect(t, out)
                stage(pair, 3)
                if t == 0:
                    whole = second_shares(shares)
                if t > 0:
                    stage(following, 2)
                stage(gather, 5)
                back = backward(t, False)
                stage(pair, 4)
                if t == last - 1:
                    stage(later, 2)
                if t > 0:
                    stage(following, 3)
            sends += back
            stage(pair, 5)
            if t == 0:
                last_shares(whole)
            finish(t, back, pair, 0)
    else:
        hidden_part(last, 128)
        opening = scatters(s.sums[steps], s.rests[0], 128, 128 + cap)
        stage(opening, 0, 1)
        act2 = act_second(last, act)
        loads[1].wait()
        carried_part(0)
        stage(opening, 2)
        out = dispatch(last, act2)
        weight_part(last, True)
        stage(opening, 3)
        for t in range(last):
            factors(t)
        stage(opening, 4)
        loads[2].wait()
        collect(last, out)
        stage(opening, 5)
        gather = slopes(last, opening, 0)
        stage(gather, 1)
        exchanged(early, s.in_early)
        hidden_part(last - 1, 128)
        pair = scatters(s.sums[last], s.rests[0], 0, 128 + cap)
        stage(pair, 0)
        for number in range(1, 5):
            stage(pair, number)
            stage(gather, number + 1)
        sends += act + act2 + out + early
        for t in range(last, -1, -1):
            if t < last:
                act = begin(t)
                pair = scatters(s.sums[t], s.rests[0], 0, 128 + cap if t > 0 else 128)
                carried_part(0)
                stage(pair, 0, 1)
                stage(gather, 3)
                act2 = act_second(t, act)
                weight_part(t, False)
                stage(pair, 2)
                stage(gather, 4)
                if t == 0:
                    shares = first_shares()
                out = dispatch(t, act2)
                stage(pair, 3)
                sends += act + act2 + out
                collect(t, out)
                stage(pair, 4)
                if t == 0:
                    whole = second_shares(shares)
                stage(gather, 5)
            back = backward(t, False)
            sends += back
            stage(pair, 5)
            if t > 0:
                gather = slopes(t - 1, pair, 128)
                stage(gather, 1)
                if t > 1:
                    hidden_part(t - 2, 128)
                stage(gather, 2)
            else:
                last_shares(whole)
            finish(t, back, pair, 0)
    start_out[...] = s.grad[...].astype(BF16)
    wait_sends(sends)


def sum_bufs(width):
    def four():
        return (
            pltpu.VMEM((2, 2, 128, width), BF16),
            pltpu.VMEM((2, RING, 128, width), BF16),
            pltpu.VMEM((2, 64, width), BF16),
            pltpu.VMEM((2, 128, width), BF16),
        )

    return four(), four()


def scratch_shapes(steps, cap, deep, groups, members, blocks):
    half = cap // 2
    held = 128 + 2 * cap if deep else 128 + cap
    v = pltpu.VMEM
    shapes = dict(
        first=v((members, blocks * 256, 256), BF16),
        recur=v((3, blocks * 256, 256), BF16),
        second=v((members * 128, blocks * 256), BF16),
        out_early=v((groups, steps - 1, PAIR, 256), BF16),
        in_early=v((groups, steps - 1, PAIR, 256), BF16),
        pack=v((groups * PAIR, 128), BF16),
        unpack=v((128, groups * PAIR), BF16),
        choose=v((cap, groups * PAIR), BF16),
        spread=v((groups * PAIR, cap), BF16),
        mask=v((members, cap, 256), BF16),
        factor=v((steps, 4, 256, 128), F32),
        bound=v((steps, 128, 128), F32),
        grad=v((256, 128), F32),
        pre=v((768, 128), BF16),
        act_own=v((steps, 2, 128, 128), BF16),
        act_in=v((steps, 2, 3, 128, 128), BF16),
        policy_out=v((steps, groups, PAIR, 128), BF16),
        policy_in=v((steps, groups, PAIR, 128), BF16),
        policy=v((cap, members * 128), BF16),
        latent=v((members * 256, cap), BF16),
        names=v((8, cap), F32),
        scaled=v((cap, blocks * 256), BF16),
        weight=v((128, 768), F32),
        share_out=v((groups, 16, 768), BF16),
        share_in=v((groups, 16, 768), BF16),
        share_all=v((groups, 16, 768), BF16),
        back=v((cap, 256), F32),
        return_out=v((steps, groups, PAIR, 256), BF16),
        return_in=v((steps, groups, PAIR, 256), BF16),
        held_a=v((RING, RING, 128, held), BF16),
        held_b=v((RING, RING, 128, held), BF16),
        slope_a=v((2, RING, RING, half, 256), BF16),
        slope_b=v((2, RING, RING, half, 256), BF16),
    )
    if deep:
        widths = [128] * steps + [cap] * steps
        rests = (cap, cap, 128)
        shapes.update(upward=v((cap, blocks * 256), F32))
    else:
        widths = [128] + [128 + cap] * (steps - 1) + [cap]
        rests = (128 + cap,)
    shapes.update(
        sums=[sum_bufs(width) for width in widths],
        rests=[[v((RING, 128, width), BF16) for side in range(2)] for width in rests],
    )
    copies = 3 * (groups - 1) + 2 * steps * 24 + steps * (16 + 6 + 2 * (groups - 1))
    shapes.update(send_sems=pltpu.SemaphoreType.DMA((copies,)))
    shapes.update(recv_sems=pltpu.SemaphoreType.DMA((copies,)))
    shapes.update(load_sems=pltpu.SemaphoreType.DMA((3,)))
    return shapes


def call(cap, deep, groups, blocks, name, collective_id):
    def run(states, gates, actions, final_grad, act_w, opp_row, late, recur, first, second):
        steps, members = states.shape[0], first.shape[0]
        vmem = pl.BlockSpec(memory_space=pltpu.VMEM)
        hbm = pl.BlockSpec(memory_space=pl.ANY)
        return pl.pallas_call(
            functools.partial(kernel, steps, cap, deep, groups, members, blocks),
            out_shape=(
                jax.ShapeDtypeStruct((256, 128), BF16),
                jax.ShapeDtypeStruct((3, 128, 256), F32),
            ),
            in_specs=[vmem] * 7 + [hbm] * 3,
            out_specs=(vmem, vmem),
            scratch_shapes=jax.tree.leaves(scratch_shapes(steps, cap, deep, groups, members, blocks)),
            compiler_params=pltpu.CompilerParams(
                collective_id=collective_id, has_side_effects=True, vmem_limit_bytes=62 << 20
            ),
            name=name,
        )(states, gates, actions, final_grad, act_w, opp_row, late, recur, first, second)

    return run


def body(
    states,
    gate_inputs,
    actions,
    final_grad,
    recur_weight,
    act_weight,
    opp_first,
    opp_second,
    opponent,
):
    groups = lax.axis_size("pop")
    blocks = lax.axis_size("unit")
    recur = jnp.transpose(recur_weight, (1, 0, 2))
    act_w = jnp.transpose(act_weight, (1, 0, 2))
    opp_row = opponent.reshape(1, -1)
    late, everyone = spread(states, opp_row, groups, opp_first.shape[0])
    operands = (
        states,
        gate_inputs,
        actions,
        final_grad,
        act_w,
        opp_row,
        late,
        recur,
        opp_first,
        opp_second.reshape(-1, opp_second.shape[2]),
    )
    everyone = everyone[:, 0, :].reshape(1, -1)
    named = everyone // opp_first.shape[0] == jnp.arange(groups, dtype=jnp.int32)[:, None]
    most = jnp.max(jnp.sum(named.astype(jnp.int32), axis=1))
    start, weight = lax.cond(
        most <= FEW,
        call(FEW, True, groups, blocks, "few_slots", 0),
        call(groups * PAIR, False, groups, blocks, "all_slots", 1),
        *operands,
    )
    return start, jnp.transpose(weight, (1, 0, 2))


def solution(mesh):
    placed = (
        P(None, "unit", "pop"),
        P(None, None, "unit", "pop"),
        P(None, None, "pop"),
        P("unit", "pop"),
        P(None, None, "unit"),
        P(None, None, "unit"),
        P("pop", None, "unit"),
        P("pop", None, None),
        P("pop", None),
    )
    return jax.shard_map(
        body,
        mesh=mesh,
        in_specs=placed,
        out_specs=(P("unit", "pop"), P(None, None, "unit")),
        check_vma=False,
    )
```
